256 devices in a mesh: gx: 4 (over x_hi, core), gy: 8 (over y, x_lo), ha: 8 (over z).
Axes of the slice: x: 4 (x_hi: 2, x_lo: 2; x = x_hi * 2 + x_lo), y: 4, z: 8, core: 2. Of those that a mesh axis runs over, the one named last changes fastest.
Arguments:
- initial_value: float32 [64, 128, 8192], P('gx', 'gy', 'ha'), may hold values from -6 to 6
- corner: int32 [256, 4, 256], P(('gx', 'gy', 'ha')), may hold values from -1 to 244670, as said below
- weights: float32 [256, 16, 4, 256], P(('gx', 'gy', 'ha')), may hold values from 0 to 0.125
Outputs:
- final_value: float32 [64, 128, 8192], P('gx', 'gy', 'ha')
- sample_values: float32 [256, 4, 256], P(('gx', 'gy', 'ha'))
The draws below stay inside these ranges and needn't reach their ends.
Inputs may be any that keep to these rules, and one draw needn't show every extreme that they name: A live corner is ((a 16 + b) * 16 + k) * 64 + v with a <= 14, b <= 14, k <= 14, v <= 62; -1 marks an empty slot; in each bucket [s, :, o] the live slots come first; in every draw some owner's buckets are full from every source.
All inputs are finite; a program needn't handle non-finite values.
Results may differ from the reference program's by a relative error of at most 0.0003.
Values sent between devices are 32-bit elements; how exact they have to be, the bound alone decides.
No kernel may reach another device: no remote copies, remote signals or barrier semaphores. Data moves between devices by JAX's collectives and lax.ppermute only.
A program may use at most 64 MiB of HBM per device.

```python
import jax
import jax.numpy as jnp
from jax import lax

CX = 16
CY = 16
CH = 16
NV = 64
STEPS = 4
CAP = 4
NX = 64
NY = 128
NH = 128
NHV = 8192
OWNERS = 256
N_GY = 8
N_HA = 8


def draw_corner(key, part):
    keys = jax.random.split(key, 7)
    bucket_fill = jax.random.randint(keys[0], (OWNERS, OWNERS), 0, CAP + 1)
    hot_owner = jax.random.randint(keys[1], (OWNERS,), 0, 4) == 0
    chosen_owner = jax.random.randint(keys[2], (), 0, OWNERS)
    hot_owner = hot_owner | (jnp.arange(OWNERS) == chosen_owner)
    bucket_fill = jnp.where(hot_owner[None, :], CAP, bucket_fill)
    empty_owner = (chosen_owner + 1) % OWNERS
    source_zero = jnp.arange(OWNERS)[:, None] == 0
    empty_mask = source_zero & (jnp.arange(OWNERS)[None, :] == empty_owner)
    bucket_fill = jnp.where(empty_mask, 0, bucket_fill)
    local_x = jax.random.randint(keys[3], (OWNERS, CAP, OWNERS), 0, CX - 1)
    local_y = jax.random.randint(keys[4], (OWNERS, CAP, OWNERS), 0, CY - 1)
    local_h = jax.random.randint(keys[5], (OWNERS, CAP, OWNERS), 0, CH - 1)
    local_v = jax.random.randint(keys[6], (OWNERS, CAP, OWNERS), 0, NV - 1)
    flat_cell = ((local_x * CY + local_y) * CH + local_h) * NV + local_v
    top_cell = (((CX - 2) * CY + CY - 2) * CH + CH - 2) * NV + NV - 2
    top_mask = (jnp.arange(OWNERS)[:, None, None] == 0) & (jnp.arange(CAP)[None, :, None] == 0) & (jnp.arange(OWNERS)[None, None, :] == chosen_owner)
    flat_cell = jnp.where(top_mask, top_cell, flat_cell)
    slot_index = jnp.arange(CAP)[None, :, None]
    live_slot = slot_index < bucket_fill[:, None, :]
    return jnp.where(live_slot, flat_cell, -1).astype(jnp.int32)


def block_scale(stream_key, extent, cuts, smallest, high):
    factor_of, own = 1.0, jax.random.fold_in(stream_key, 6)
    for dim, parts in cuts:
        draws = jnp.exp(jax.random.uniform(jax.random.fold_in(own, dim), (parts,), jnp.float32, smallest / len(cuts), high / len(cuts)))
        factor_of = factor_of * jnp.repeat(draws, extent[dim] // parts).reshape([-1 if axis == dim else 1 for axis in range(len(extent))])
    return factor_of


def noise(stream_key, extent, spread, reach, shards=(), kind=jnp.bfloat16):
    gain = block_scale(stream_key, extent, shards, -0.22, 0.18) if shards else 1.0
    drawn = jax.random.normal(stream_key, extent, jnp.float32) * spread * gain
    return jnp.minimum(jnp.maximum(drawn, -reach), reach).astype(kind)


def setup_inputs(seed: int = 0) -> dict:
    key_of = jax.random.split(jax.random.key(seed), 4)
    initial_value = noise(key_of[0], (NX, NY, NHV), 1.0, 6.0, ((0, 4), (1, 8), (2, 8)), jnp.float32)
    corner = draw_corner(jax.random.fold_in(key_of[3], 71), 0)
    weights = jnp.clip(0.125 * jax.random.uniform(key_of[2], (OWNERS, 16, CAP, OWNERS), jnp.float32) ** block_scale(key_of[2], (OWNERS, 16, CAP, OWNERS), ((0, 256),), -0.2, 0.2), 0.0, 0.125)
    return {"initial_value": initial_value, "corner": corner, "weights": weights}


epsilon = 1e-6
turn_rate = 1.0
time_step = 0.15
two_pi = 6.283185307179586


def window_of(array_in, begin_at, length_of, along, stride):
    return lax.slice_in_dim(array_in, begin_at * stride, (begin_at + length_of) * stride, axis=along)


def blend(outer_low, inner_low, center, inner_high, outer_high):
    guess_one = outer_low / 3.0 - 7.0 * inner_low / 6.0 + 11.0 * center / 6.0
    guess_two = -inner_low / 6.0 + 5.0 * center / 6.0 + inner_high / 3.0
    guess_three = center / 3.0 + 5.0 * inner_high / 6.0 - outer_high / 6.0
    rough_one = 13.0 / 12.0 * (outer_low - 2.0 * inner_low + center) ** 2 + 0.25 * (outer_low - 4.0 * inner_low + 3.0 * center) ** 2
    rough_two = 13.0 / 12.0 * (inner_low - 2.0 * center + inner_high) ** 2 + 0.25 * (inner_low - inner_high) ** 2
    rough_three = 13.0 / 12.0 * (center - 2.0 * inner_high + outer_high) ** 2 + 0.25 * (3.0 * center - 4.0 * inner_high + outer_high) ** 2
    weight_one = 0.1 / (rough_one + epsilon) ** 2
    weight_two = 0.6 / (rough_two + epsilon) ** 2
    weight_three = 0.3 / (rough_three + epsilon) ** 2
    return (weight_one * guess_one + weight_two * guess_two + weight_three * guess_three) / (weight_one + weight_two + weight_three)


def weno_pair(padded, along, stride, length_of):
    differences = window_of(padded, 1, length_of + 5, along, stride) - window_of(padded, 0, length_of + 5, along, stride)
    stencil = [window_of(differences, shift_at, length_of, along, stride) for shift_at in range(6)]
    slope_minus = blend(stencil[0], stencil[1], stencil[2], stencil[3], stencil[4])
    slope_plus = blend(stencil[5], stencil[4], stencil[3], stencil[2], stencil[1])
    return slope_minus, slope_plus


def drift_tables(first_heading, count_h, total_h):
    heading_index = first_heading + jnp.arange(count_h, dtype=jnp.int32)
    heading_angle = heading_index.astype(jnp.float32) * (two_pi / total_h)
    speeds = 0.5 + jnp.arange(NV, dtype=jnp.int32).astype(jnp.float32) / (NV - 1)
    drift_x = (jnp.cos(heading_angle)[:, None] * speeds[None, :]).reshape(-1)
    drift_y = (jnp.sin(heading_angle)[:, None] * speeds[None, :]).reshape(-1)
    return drift_x, drift_y


def advance(level_set, padded_x, padded_y, padded_h, drift_x, drift_y):
    count_x = level_set.shape[0]
    count_y = level_set.shape[1]
    count_h = level_set.shape[2] // NV
    xm_slope, xp_slope = weno_pair(padded_x, 0, 1, count_x)
    ym_slope, yp_slope = weno_pair(padded_y, 1, 1, count_y)
    hm_slope, hp_slope = weno_pair(padded_h, 2, NV, count_h)
    hamiltonian = drift_x * (0.5 * (xm_slope + xp_slope)) + drift_y * (0.5 * (ym_slope + yp_slope))
    hamiltonian = hamiltonian - turn_rate * jnp.abs(0.5 * (hm_slope + hp_slope))
    hamiltonian = hamiltonian - 0.5 * (jnp.abs(drift_x) * (xp_slope - xm_slope) + jnp.abs(drift_y) * (yp_slope - ym_slope) + turn_rate * (hp_slope - hm_slope))
    return level_set - time_step * jnp.maximum(hamiltonian, 0.0)


def reference(initial_value, corner, weights):
    drift_x, drift_y = drift_tables(0, NH, NH)
    level_set = initial_value
    for step_index in range(STEPS):
        padded_x = jnp.pad(level_set, ((3, 3), (0, 0), (0, 0)))
        padded_y = jnp.pad(level_set, ((0, 0), (3, 3), (0, 0)))
        padded_h = jnp.concatenate([level_set[:, :, NHV - 3 * NV:], level_set, level_set[:, :, :3 * NV]], axis=2)
        level_set = advance(level_set, padded_x, padded_y, padded_h, drift_x, drift_y)
    owners = jnp.arange(OWNERS, dtype=jnp.int32)
    owner_x = owners // (N_GY * N_HA)
    owner_y = (owners // N_HA) % N_GY
    owner_h = owners % N_HA
    live_slot = corner >= 0
    clamped = jnp.maximum(corner, 0)
    local_x = clamped // (CY * CH * NV)
    local_y = (clamped // (CH * NV)) % CY
    local_h = (clamped // NV) % CH
    local_v = clamped % NV
    base_index = ((owner_x[None, None, :] * CX + local_x) * NY + owner_y[None, None, :] * CY + local_y) * NHV
    base_index = base_index + (owner_h[None, None, :] * CH + local_h) * NV + local_v
    offset_list = []
    for bit_x in range(2):
        for bit_y in range(2):
            for bit_h in range(2):
                for bit_v in range(2):
                    offset_list.append(bit_x * NY * NHV + bit_y * NHV + bit_h * NV + bit_v)
    corner_offsets = jnp.array(offset_list, dtype=jnp.int32)
    flat_grid = level_set.reshape(-1)
    gathered = flat_grid[base_index[None] + corner_offsets[:, None, None, None]]
    weight_table = jnp.moveaxis(weights, 1, 0)
    sampled = jnp.sum(weight_table * gathered, axis=0)
    sample_values = jnp.where(live_slot, sampled, 0.0)
    return level_set, sample_values
```

```python
import functools

import jax
import jax.numpy as jnp
import numpy as np
from jax import lax
from jax.experimental import pallas as pl
from jax.experimental.pallas import tpu as pltpu
from jax.sharding import PartitionSpec as P

NV = 64
STEPS = 4
EPS = 1e-06
DT = 0.15
CX = CY = CH = 16
PAIRS = CH // 2
ROWS = CX * CY * PAIRS
XROW = CY * PAIRS
YROW = PAIRS
F32 = jnp.float32
VMEM = pl.BlockSpec(memory_space=pltpu.VMEM)
SMEM = pl.BlockSpec(memory_space=pltpu.SMEM)
ALL = ("gx", "gy", "ha")

X0, XD, XFA, XFB, XHA, XHB, Y0, YD, YFA, YFB, YHA, YHB, HFA, HFB, HHA, HHB = range(16)


def smooth(low, high, turn):
    mid = (turn * (4.0 / 3.0)) * turn + low * high + EPS
    twice = turn + turn
    return mid + high * twice, mid, mid - low * twice


def inverse(d):
    r = pl.reciprocal(d, approx=True)
    return r * (2.0 - d * r)


def upwind(cells):
    count = len(cells) - 5
    diff = [cells[n + 1] - cells[n] for n in range(count + 4)]
    curve = [diff[n + 1] - diff[n] for n in range(count + 3)]
    turn = [curve[n + 1] - curve[n] for n in range(count + 2)]
    bend = [turn[n] - turn[n + 1] for n in range(count + 1)]
    terms = [smooth(curve[n], curve[n + 1], turn[n]) for n in range(count + 2)]
    slopes = []
    for n in range(count):
        a, b, c = terms[n][0], terms[n + 1][1], terms[n + 2][2]
        bc, ac, ab = b * c, a * c, a * b
        alpha, beta, gamma = bc * bc, ac * ac, ab * ab
        gamma3 = 3.0 * gamma
        down = alpha + 6.0 * beta + gamma3
        up = alpha * (bend[n] + bend[n]) + gamma3 * bend[n + 1]
        inner = curve[n + 1] + (curve[n + 2] + curve[n + 2]) + up * inverse(down)
        slopes.append(diff[n + 2] + inner * (1.0 / 6.0))
    return slopes


def heading_terms(pairs, first_half):
    def odd(low, high):
        return jnp.where(first_half, low, high)

    count = len(pairs)
    turned = [pltpu.roll(p, NV, 1) for p in pairs]
    between = [odd(turned[n], turned[n + 1]) for n in range(count - 1)]
    diff_e = [between[n] - pairs[n] for n in range(count - 1)]
    diff_o = [pairs[n + 1] - between[n] for n in range(count - 1)]
    curve_e = [diff_o[n] - diff_e[n] for n in range(count - 1)]
    curve_o = [diff_e[n + 1] - diff_o[n] for n in range(count - 2)]
    turn_e = [curve_o[n] - curve_e[n] for n in range(count - 2)]
    turn_o = [curve_e[n + 1] - curve_o[n] for n in range(count - 2)]
    terms = [smooth(curve_e[n], curve_o[n], turn_e[n]) for n in range(count - 2)]
    mid_turned = [pltpu.roll(t[1], NV, 1) for t in terms]
    minus, plus = [None], [None]
    for n in range(1, count - 2):
        a, c = terms[n - 1][0], terms[n][2]
        b = odd(mid_turned[n - 1], mid_turned[n])
        bc, ac, ab = b * c, a * c, a * b
        alpha, beta, gamma = bc * bc, ac * ac, ab * ab
        bend_a = alpha * (turn_e[n - 1] - turn_o[n - 1])
        bend_c = gamma * (turn_o[n - 1] - turn_e[n])
        both = alpha + gamma
        shared = both + 6.0 * beta
        bends = bend_a + bend_c
        bends = bends + bends
        before, here = curve_o[n - 1], curve_e[n]
        sums = before + here
        down = shared + (gamma + gamma)
        inner = sums + here + (bends + bend_c) * inverse(down)
        minus.append(pltpu.roll(diff_e[n] + inner * (1.0 / 6.0), NV, 1))
        if n >= 2:
            down = shared + (alpha + alpha)
            inner = sums + before + (bends + bend_a) * inverse(down)
            plus.append(inner * (1.0 / 6.0) - diff_e[n])
        else:
            plus.append(None)
    return [
        jnp.minimum(odd(minus[n - 1], minus[n]), plus[n]) for n in range(2, count - 2)
    ]


def tile(ref, row):
    return ref[pl.ds(pl.multiple_of(row, 8), 8), :]


def put(ref, row, value):
    ref[pl.ds(pl.multiple_of(row, 8), 8), :] = value


def lanes_first_half():
    return lax.broadcasted_iota(jnp.int32, (8, 128), 1) < NV


def write_faces(prm, v_ref, faces):
    fxa, fxb, fya, fyb, fha, fhb = faces

    def body(n, _):
        for l in range(3):
            put(fxa, l * XROW + n * YROW, tile(v_ref, (prm[XFA] + l) * XROW + n * YROW))
            put(fxb, l * XROW + n * YROW, tile(v_ref, (prm[XFB] + l) * XROW + n * YROW))
            put(fya, l * XROW + n * YROW, tile(v_ref, n * XROW + (prm[YFA] + l) * YROW))
            put(fyb, l * XROW + n * YROW, tile(v_ref, n * XROW + (prm[YFB] + l) * YROW))
        for l in range(2):
            for t in range(2):
                base = n * XROW + t * 64
                out = (l * 32 + n * 2 + t) * 8
                put(fha, out, v_ref[pl.ds(base + prm[HFA] + l, 8, stride=8), :])
                put(fhb, out, v_ref[pl.ds(base + prm[HFB] + l, 8, stride=8), :])
        return 0

    lax.fori_loop(0, 16, body, 0)


def faces_kernel(prm, v_ref, *faces):
    write_faces(prm, v_ref, faces)


def line_cells(prm, v_ref, start, direction, stride, offset, first, last):
    return [
        tile(v_ref, (prm[start] + prm[direction] * i) * stride + offset)
        for i in range(first, last)
    ]


def inner_kernel(prm, v_ref, adx_ref, ady_ref, h_ref):
    first_half = lanes_first_half()
    adx, ady = adx_ref[...], ady_ref[...]
    zero = jnp.zeros((8, 128), F32)

    def along_x(y, _):
        slopes = upwind(line_cells(prm, v_ref, X0, XD, XROW, y * YROW, 0, 16))
        for i in range(16):
            row = (prm[X0] + prm[XD] * i) * XROW + y * YROW
            put(h_ref, row, adx * slopes[i - 3] if 3 <= i <= 13 else zero)
        return 0

    lax.fori_loop(0, 16, along_x, 0)

    def along_y(x, _):
        slopes = upwind(line_cells(prm, v_ref, Y0, YD, YROW, x * XROW, 0, 16))
        for i in range(3, 14):
            row = (prm[Y0] + prm[YD] * i) * YROW + x * XROW
            put(h_ref, row, tile(h_ref, row) + ady * slopes[i - 3])
        return 0

    lax.fori_loop(0, 16, along_y, 0)

    def along_h(n, _):
        base = n * 64
        pairs = [v_ref[pl.ds(base + p, 8, stride=8), :] for p in range(8)]
        for p, term in enumerate(heading_terms(pairs, first_half)):
            at = pl.ds(base + 2 + p, 8, stride=8)
            h_ref[at, :] = h_ref[at, :] + term
        return 0

    lax.fori_loop(0, 32, along_h, 0)


def outer_kernel(
    last, prm, v_ref, h_in, adx_ref, ady_ref, rxa, rxb, rya, ryb, rha, rhb, out_ref, *rest
):
    faces, (xs, ys, hs, h_ref) = rest[:-4], rest[-4:]
    first_half = lanes_first_half()
    adx, ady = adx_ref[...], ady_ref[...]

    def halos(n, _):
        for l in range(3):
            src = l * XROW + n * YROW
            put(xs, (prm[XHA] + prm[XD] * l) * XROW + n * YROW, tile(rxa, src))
            put(xs, (prm[XHB] + prm[XD] * l) * XROW + n * YROW, tile(rxb, src))
            put(ys, (prm[YHA] + prm[YD] * l) * XROW + n * YROW, tile(rya, src))
            put(ys, (prm[YHB] + prm[YD] * l) * XROW + n * YROW, tile(ryb, src))
        for l in range(2):
            for t in range(2):
                at = (n * 2 + t) * 8
                put(hs, (prm[HHA] + l) * 256 + at, tile(rha, l * 256 + at))
                put(hs, (prm[HHB] + l) * 256 + at, tile(rhb, l * 256 + at))
        return 0

    lax.fori_loop(0, 16, halos, 0)

    def along_x(y, _):
        at = y * YROW
        cells = [tile(xs, l * XROW + at) for l in range(3)]
        cells += line_cells(prm, v_ref, X0, XD, XROW, at, 0, 5)
        low = upwind(cells)
        cells = line_cells(prm, v_ref, X0, XD, XROW, at, 11, 16)
        cells += [tile(xs, l * XROW + at) for l in range(3, 5)]
        high = upwind(cells)
        for i, slope in list(zip(range(3), low)) + list(zip(range(14, 16), high)):
            row = (prm[X0] + prm[XD] * i) * XROW + at
            put(h_ref, row, tile(h_in, row) + adx * slope)
        for i in range(3, 14):
            row = (prm[X0] + prm[XD] * i) * XROW + at
            put(h_ref, row, tile(h_in, row))
        return 0

    lax.fori_loop(0, 16, along_x, 0)

    def along_y(x, _):
        at = x * YROW
        cells = [tile(ys, l * XROW + at) for l in range(3)]
        cells += line_cells(prm, v_ref, Y0, YD, YROW, x * XROW, 0, 5)
        low = upwind(cells)
        cells = line_cells(prm, v_ref, Y0, YD, YROW, x * XROW, 11, 16)
        cells += [tile(ys, l * XROW + at) for l in range(3, 5)]
        high = upwind(cells)
        for i, slope in list(zip(range(3), low)) + list(zip(range(14, 16), high)):
            row = (prm[Y0] + prm[YD] * i) * YROW + x * XROW
            put(h_ref, row, tile(h_ref, row) + ady * slope)
        return 0

    lax.fori_loop(0, 16, along_y, 0)

    def along_h(n, _):
        base = n * 64
        own = [v_ref[pl.ds(base + p, 8, stride=8), :] for p in range(8)]
        ring = [tile(hs, l * 256 + n * 8) for l in range(4)]
        low = heading_terms(ring[:2] + own[:4], first_half)
        high = heading_terms(own[4:] + ring[2:], first_half)
        for p in range(8):
            at = pl.ds(base + p, 8, stride=8)
            total = h_ref[at, :]
            if p < 2:
                total = total + low[p]
            if p > 5:
                total = total + high[p - 6]
            out_ref[at, :] = own[p] - DT * jnp.maximum(total, 0.0)
        return 0

    lax.fori_loop(0, 32, along_h, 0)
    if not last:
        write_faces(prm, out_ref, faces)


def call(body, name, outs, in_specs, scratch=(), flops=0, moved=4 << 20):
    return pl.pallas_call(
        body,
        name=name,
        out_shape=[jax.ShapeDtypeStruct(s, F32) for s in outs],
        in_specs=in_specs,
        out_specs=[VMEM] * len(outs),
        scratch_shapes=[pltpu.VMEM(s, F32) for s in scratch],
        cost_estimate=pl.CostEstimate(flops=flops, bytes_accessed=moved, transcendentals=0),
        compiler_params=pltpu.CompilerParams(vmem_limit_bytes=40 << 20),
    )


FACES = [(3 * XROW, 128)] * 4 + [(512, 128)] * 2
BLOCK = (ROWS, 128)


def exchange(faces):
    sides = (("gx", 0, False), ("gx", 1, False), ("gy", 0, False), ("gy", 1, False), ("ha", 0, True), ("ha", 1, True))
    arrived = []
    for face, (axis, offset, closed) in zip(faces, sides):
        count = lax.axis_size(axis)
        pairs = []
        for i in range(offset, count if closed else count - 1, 2):
            pairs += [(i, (i + 1) % count), ((i + 1) % count, i)]
        arrived.append(lax.ppermute(face, axis, pairs))
    return arrived


def drift_tables(blocks):
    angle = np.arange(blocks * CH) * (2.0 * np.pi / (blocks * CH))
    speeds = 0.5 + np.arange(NV) / (NV - 1)
    tables, signs = [], []
    for part in (np.cos(angle), np.sin(angle)):
        part = np.where(np.abs(part) < 1e-12, 0.0, part).reshape(blocks, CH)
        positive = (part >= 0).all(axis=1)
        assert (positive | (part <= 0).all(axis=1)).all()
        tables.append(np.abs(part[:, :, None] * speeds).reshape(blocks, PAIRS, 2 * NV).astype(np.float32))
        signs.append(np.where(positive, 1, -1))
    return tables, signs


def parameters(signs):
    gx, gy, ha = (lax.axis_index(a) for a in ALL)
    table = []
    for index, sign in ((gx, signs[0]), (gy, signs[1])):
        even = index % 2 == 0
        wind = jnp.asarray(sign, jnp.int32)[ha]
        high = jnp.where(wind > 0, 3, 2)
        low = jnp.where(wind > 0, 0, 5)
        table += [
            jnp.where(wind > 0, 0, 15),
            wind,
            jnp.where(even, 13, 0),
            jnp.where(even, 0, 13),
            jnp.where(even, high, low),
            jnp.where(even, low, high),
        ]
    even = ha % 2 == 0
    table += [jnp.where(even, 6, 0), jnp.where(even, 0, 6), jnp.where(even, 2, 0), jnp.where(even, 0, 2)]
    return jnp.stack([jnp.asarray(t, jnp.int32) for t in table])


def steps(initial_value, request):
    tables, signs = drift_tables(lax.axis_size("ha"))
    ha = lax.axis_index("ha")
    adx, ady = (jnp.asarray(t)[ha] for t in tables)
    prm = parameters(signs)
    value = initial_value.reshape(BLOCK)
    faces = call(faces_kernel, "faces", FACES, [SMEM, VMEM])(prm, value)
    for step in range(STEPS):
        last = step == STEPS - 1
        arrived = exchange(faces)
        if step < 3:
            request = lax.all_to_all(request, ALL[step], split_axis=step, concat_axis=step, tiled=True)
            request, arrived = lax.optimization_barrier((request, arrived))
        (part,) = call(inner_kernel, "inner", [BLOCK], [SMEM] + [VMEM] * 3, flops=30_000_000)(prm, value, adx, ady)
        out = call(
            functools.partial(outer_kernel, last),
            "outer",
            [BLOCK] + ([] if last else FACES),
            [SMEM] + [VMEM] * 10,
            scratch=[(6 * XROW, 128), (6 * XROW, 128), (4 * 256, 128), BLOCK],
            flops=15_000_000,
        )(prm, value, part, adx, ady, *arrived)
        value, faces = out[0], out[1:]
        if step < 2:
            faces, request = lax.optimization_barrier((faces, request))
    return value, request


def sample_kernel(rows_ref, v_ref, w_ref, out_ref, table, picked):
    first_half = lanes_first_half()

    def fill(n, _):
        pair = tile(v_ref, n * 8)
        turned = pltpu.roll(pair, NV, 1)
        between = jnp.where(first_half, turned, pltpu.roll(turned, 7, 0))
        table[pl.ds(n * 16, 8, stride=2), :] = pair
        table[pl.ds(n * 16 + 1, 8, stride=2), :] = between
        return 0

    lax.fori_loop(0, CX * CY, fill, 0)

    def pick(n, _):
        for u in range(8):
            s = n * 8 + u
            for j in range(4):
                row = rows_ref[s * 4 + j]
                for q, shift in enumerate((0, CH, CY * CH, CY * CH + CH)):
                    picked[pl.ds((q * 4 + j) * 256 + s, 1), :] = table[pl.ds(row + shift, 1), :]
        return 0

    lax.fori_loop(0, 32, pick, 0)
    lane = lax.broadcasted_iota(jnp.int32, (8, 128), 1)
    slot = lane & 3
    corner_shift = ((lane >> 2) & 1) + NV * ((lane >> 3) & 1)

    def weigh(n, _):
        w = tile(w_ref, n * 8)
        speeds = jnp.maximum(jnp.take_along_axis(w, 64 + slot, axis=1), 0.0).astype(jnp.int32) & (NV - 1)
        total = jnp.zeros((8, 128), F32)
        for j in range(4):
            at = jnp.take_along_axis(speeds, jnp.full((8, 128), j, jnp.int32), axis=1) + corner_shift
            for q in range(4):
                read = jnp.take_along_axis(tile(picked, (q * 4 + j) * 256 + n * 8), at, axis=1)
                total = jnp.where((slot == j) & ((lane >> 4) == q), read, total)
        total = total * w
        total = jnp.where(lane < 64, total, 0.0)
        for shift in (96, 112, 120, 124):
            total = total + pltpu.roll(total, shift, 1)
        out_ref[pl.ds(n * 8, 8), :] = total[:, :4]
        return 0

    lax.fori_loop(0, 32, weigh, 0)


def local(initial_value, corner, weights):
    slots = corner.shape[1]
    owners = corner.shape[2]
    sizes = [lax.axis_size(a) for a in ALL]
    request = jnp.concatenate(
        [weights.reshape(16 * slots, owners), corner.reshape(slots, owners).astype(F32)], axis=0
    )
    request = jnp.pad(request.T, ((0, 0), (0, 128 - 17 * slots))).reshape(*sizes, 128)
    value, request = steps(initial_value, request)
    request = request.reshape(owners, 128)
    codes = jnp.maximum(request[:, 64 : 64 + slots], 0.0).astype(jnp.int32).reshape(-1)
    (sums,) = call(
        sample_kernel,
        "samples",
        [(owners, slots)],
        [SMEM, VMEM, VMEM],
        scratch=[(2 * ROWS, 128), (16 * owners, 128)],
    )(codes // NV, value, request)
    sampled = lax.all_to_all(sums, ALL, split_axis=0, concat_axis=0, tiled=True)
    sampled = jnp.where(corner >= 0, sampled.T.reshape(corner.shape), 0.0)
    return value.reshape(initial_value.shape), sampled


def solution(mesh):
    return jax.shard_map(
        local,
        mesh=mesh,
        in_specs=(
            P("gx", "gy", "ha"),
            P(("gx", "gy", "ha"), None, None),
            P(("gx", "gy", "ha"), None, None, None),
        ),
        out_specs=(P("gx", "gy", "ha"), P(("gx", "gy", "ha"), None, None)),
        check_vma=False,
    )
```

```python
import functools

import jax
import jax.numpy as jnp
import numpy as np
from jax import lax
from jax.experimental import pallas as pl
from jax.experimental.pallas import tpu as pltpu
from jax.sharding import PartitionSpec as P

NV = 64
STEPS = 4
EPS = 1e-06
DT = 0.15
CX = CY = CH = 16
PAIRS = CH // 2
ROWS = CX * CY * PAIRS
XROW = CY * PAIRS
YROW = PAIRS
F32 = jnp.float32
VMEM = pl.BlockSpec(memory_space=pltpu.VMEM)
SMEM = pl.BlockSpec(memory_space=pltpu.SMEM)
ALL = ("gx", "gy", "ha")

def smooth(low, high, turn):
    mid = (turn * (4.0 / 3.0)) * turn + low * high + EPS
    twice = turn + turn
    return mid + high * twice, mid, mid - low * twice


def inverse(d):
    r = pl.reciprocal(d, approx=True)
    return r * (2.0 - d * r)


def upwind(cells):
    count = len(cells) - 5
    diff = [cells[n + 1] - cells[n] for n in range(count + 4)]
    curve = [diff[n + 1] - diff[n] for n in range(count + 3)]
    turn = [curve[n + 1] - curve[n] for n in range(count + 2)]
    bend = [turn[n] - turn[n + 1] for n in range(count + 1)]
    terms = [smooth(curve[n], curve[n + 1], turn[n]) for n in range(count + 2)]
    slopes = []
    for n in range(count):
        a, b, c = terms[n][0], terms[n + 1][1], terms[n + 2][2]
        bc, ac, ab = b * c, a * c, a * b
        alpha, beta, gamma = bc * bc, ac * ac, ab * ab
        gamma3 = 3.0 * gamma
        down = alpha + 6.0 * beta + gamma3
        up = alpha * (bend[n] + bend[n]) + gamma3 * bend[n + 1]
        inner = curve[n + 1] + (curve[n + 2] + curve[n + 2]) + up * inverse(down)
        slopes.append(diff[n + 2] + inner * (1.0 / 6.0))
    return slopes


def heading_terms(pairs, turned, first_half):
    count = len(pairs)
    between = [jnp.where(first_half, turned[n], turned[n + 1]) for n in range(count - 1)]
    diff_e = [between[n] - pairs[n] for n in range(count - 1)]
    diff_o = [pairs[n + 1] - between[n] for n in range(count - 1)]
    curve_e = [diff_o[n] - diff_e[n] for n in range(count - 1)]
    curve_o = [diff_e[n + 1] - diff_o[n] for n in range(count - 2)]
    turn_e = [curve_o[n] - curve_e[n] for n in range(count - 2)]
    turn_o = [curve_e[n + 1] - curve_o[n] for n in range(count - 2)]
    even = [smooth(curve_e[n], curve_o[n], turn_e[n]) for n in range(count - 2)]
    odd = [smooth(curve_o[n], curve_e[n + 1], turn_o[n]) for n in range(count - 2)]

    def inner_sum(a, b, c, before, here, bend_a, bend_c):
        bc, ac, ab = b * c, a * c, a * b
        alpha, beta, gamma = bc * bc, ac * ac, ab * ab
        gamma3 = 3.0 * gamma
        down = alpha + 6.0 * beta + gamma3
        up = alpha * (bend_a + bend_a) + gamma3 * bend_c
        return before + (here + here) + up * inverse(down)

    result = []
    for n in range(2, count - 2):
        bend_m, bend_0, bend_p = (
            turn_o[n - 2] - turn_e[n - 1],
            turn_e[n - 1] - turn_o[n - 1],
            turn_o[n - 1] - turn_e[n],
        )
        minus = inner_sum(
            odd[n - 2][0], even[n - 1][1], odd[n - 1][2], curve_e[n - 1], curve_o[n - 1], bend_m, bend_0
        )
        plus = inner_sum(
            even[n][2], odd[n - 1][1], even[n - 1][0], curve_e[n], curve_o[n - 1], bend_p, bend_0
        )
        sixth = 1.0 / 6.0
        result.append(jnp.minimum(diff_o[n - 1] + minus * sixth, plus * sixth - diff_e[n]))
    return result


def tile(ref, row):
    return ref[pl.ds(pl.multiple_of(row, 8), 8), :]


def put(ref, row, value):
    ref[pl.ds(pl.multiple_of(row, 8), 8), :] = value


def lanes_first_half():
    return lax.broadcasted_iota(jnp.int32, (8, 128), 1) < NV


def scalars(signs):
    ha = lax.axis_index("ha")
    found = []
    for axis, sign in (("gx", signs[0]), ("gy", signs[1])):
        even = lax.rem(lax.axis_index(axis), 2) == 0
        wind = jnp.int32(int(sign[0]))
        for block in range(1, len(sign)):
            wind = jnp.where(ha == block, jnp.int32(int(sign[block])), wind)
        ahead = wind > 0
        high, low = jnp.where(ahead, 3, 2), jnp.where(ahead, 0, 5)
        found.append(
            (
                jnp.where(ahead, 0, 15),
                wind,
                jnp.where(even, 13, 0),
                jnp.where(even, 0, 13),
                jnp.where(even, high, low),
                jnp.where(even, low, high),
            )
        )
    even = lax.rem(ha, 2) == 0
    found.append(
        (jnp.where(even, 6, 0), jnp.where(even, 0, 6), jnp.where(even, 2, 0), jnp.where(even, 0, 2))
    )
    return found


def write_faces(where, v_ref, faces):
    (_, _, fx_a, fx_b, _, _), (_, _, fy_a, fy_b, _, _), (fh_a, fh_b, _, _) = where
    fxa, fxb, fya, fyb, fha, fhb = faces

    def body(n, _):
        for l in range(3):
            put(fxa, l * XROW + n * YROW, tile(v_ref, (fx_a + l) * XROW + n * YROW))
            put(fxb, l * XROW + n * YROW, tile(v_ref, (fx_b + l) * XROW + n * YROW))
            put(fya, l * XROW + n * YROW, tile(v_ref, n * XROW + (fy_a + l) * YROW))
            put(fyb, l * XROW + n * YROW, tile(v_ref, n * XROW + (fy_b + l) * YROW))
        for l in range(2):
            for t in range(2):
                base = n * XROW + t * 64
                out = (l * 32 + n * 2 + t) * 8
                put(fha, out, v_ref[pl.ds(base + fh_a + l, 8, stride=8), :])
                put(fhb, out, v_ref[pl.ds(base + fh_b + l, 8, stride=8), :])
        return 0

    lax.fori_loop(0, 16, body, 0, unroll=2)


def native(x, t, p):
    return x, pl.ds(8 * t, 8), pl.ds(128 * p, 128)


def first_kernel(signs, in_ref, v_ref, *faces):
    def body(x, _):
        for t in range(2):
            for p in range(8):
                v_ref[pl.ds(x * XROW + t * 64 + p, 8, stride=8), :] = in_ref[native(x, t, p)]
        return 0

    lax.fori_loop(0, 16, body, 0)
    write_faces(scalars(signs), v_ref, faces)


def inner_kernel(signs, v_ref, adx_ref, ady_ref, h_ref, turned_ref):
    (x_start, x_dir, *_), (y_start, y_dir, *_), _ = scalars(signs)
    first_half = lanes_first_half()
    adx, ady = adx_ref[...], ady_ref[...]
    zero = jnp.zeros((8, 128), F32)
    turned_ref[...] = pltpu.roll(v_ref[...], NV, 1)
    xs = [(x_start + x_dir * i) * XROW for i in range(16)]
    ys = [(y_start + y_dir * i) * YROW for i in range(16)]

    def along_x(y, _):
        slopes = upwind([tile(v_ref, row + y * YROW) for row in xs])
        for i in range(16):
            put(h_ref, xs[i] + y * YROW, adx * slopes[i - 3] if 3 <= i <= 13 else zero)
        return 0

    lax.fori_loop(0, 16, along_x, 0)

    def along_y(x, _):
        slopes = upwind([tile(v_ref, row + x * XROW) for row in ys])
        for i in range(3, 14):
            row = ys[i] + x * XROW
            put(h_ref, row, tile(h_ref, row) + ady * slopes[i - 3])
        return 0

    lax.fori_loop(0, 16, along_y, 0)

    def along_h(n, _):
        at = [pl.ds(n * 64 + p, 8, stride=8) for p in range(8)]
        terms = heading_terms([v_ref[a, :] for a in at], [turned_ref[a, :] for a in at], first_half)
        for a, term in zip(at[2:6], terms):
            h_ref[a, :] = h_ref[a, :] + term
        return 0

    lax.fori_loop(0, 32, along_h, 0)


def outer_kernel(
    signs, last, v_ref, h_in, turned_ref, adx_ref, ady_ref, rxa, rxb, rya, ryb, rha, rhb, *rest
):
    out_ref, others = rest[0], rest[1:-5]
    xs, ys, hs, hs_turned, h_ref = rest[-5:]
    where = scalars(signs)
    (x_start, x_dir, _, _, xh_a, xh_b), (y_start, y_dir, _, _, yh_a, yh_b), (_, _, hh_a, hh_b) = where
    first_half = lanes_first_half()
    adx, ady = adx_ref[...], ady_ref[...]
    for l in range(2):
        hs[pl.ds(pl.multiple_of((hh_a + l) * 256, 256), 256), :] = rha[pl.ds(l * 256, 256), :]
        hs[pl.ds(pl.multiple_of((hh_b + l) * 256, 256), 256), :] = rhb[pl.ds(l * 256, 256), :]
    hs_turned[...] = pltpu.roll(hs[...], NV, 1)
    for l in range(3):
        part = pl.ds(l * XROW, XROW)
        for ref, got, base, step in (
            (xs, rxa, xh_a, x_dir),
            (xs, rxb, xh_b, x_dir),
            (ys, rya, yh_a, y_dir),
            (ys, ryb, yh_b, y_dir),
        ):
            ref[pl.ds(pl.multiple_of((base + step * l) * XROW, XROW), XROW), :] = got[part, :]
    x_rows = [(x_start + x_dir * i) * XROW for i in range(16)]
    y_rows = [(y_start + y_dir * i) * YROW for i in range(16)]

    def edges(halo, at, rows, offset):
        own = {i: tile(v_ref, rows[i] + offset) for i in (0, 1, 2, 3, 4, 11, 12, 13, 14, 15)}
        ring = [tile(halo, l * XROW + at) for l in range(5)]
        low = upwind(ring[:3] + [own[i] for i in range(5)])
        high = upwind([own[i] for i in range(11, 16)] + ring[3:])
        return list(zip(range(3), low)) + list(zip(range(14, 16), high))

    def along_x(y, _):
        at = y * YROW
        for i, slope in edges(xs, at, x_rows, at):
            put(h_ref, x_rows[i] + at, tile(h_in, x_rows[i] + at) + adx * slope)
        for i in range(3, 14):
            put(h_ref, x_rows[i] + at, tile(h_in, x_rows[i] + at))
        return 0

    lax.fori_loop(0, 16, along_x, 0)

    def along_y(x, _):
        for i, slope in edges(ys, x * YROW, y_rows, x * XROW):
            row = y_rows[i] + x * XROW
            put(h_ref, row, tile(h_ref, row) + ady * slope)
        return 0

    lax.fori_loop(0, 16, along_y, 0)

    def along_h(n, _):
        at = [pl.ds(n * 64 + p, 8, stride=8) for p in range(8)]
        own = [v_ref[a, :] for a in at]
        own_turned = [turned_ref[a, :] for a in at]
        ring = [tile(hs, l * 256 + n * 8) for l in range(4)]
        ring_turned = [tile(hs_turned, l * 256 + n * 8) for l in range(4)]
        low = heading_terms(ring[:2] + own[:4], ring_turned[:2] + own_turned[:4], first_half)
        high = heading_terms(own[4:] + ring[2:], own_turned[4:] + ring_turned[2:], first_half)
        for p in range(8):
            total = h_ref[at[p], :]
            if p < 2:
                total = total + low[p]
            if p > 5:
                total = total + high[p - 6]
            value = own[p] - DT * jnp.maximum(total, 0.0)
            out_ref[at[p], :] = value
            if last:
                others[0][native(n // 2, lax.rem(n, 2), p)] = value
        return 0

    lax.fori_loop(0, 32, along_h, 0)
    if not last:
        write_faces(where, out_ref, others)


def call(body, name, outs, in_specs, scratch=(), flops=0, moved=4 << 20):
    return pl.pallas_call(
        body,
        name=name,
        out_shape=[jax.ShapeDtypeStruct(s, F32) for s in outs],
        in_specs=in_specs,
        out_specs=[VMEM] * len(outs),
        scratch_shapes=[pltpu.VMEM(s, F32) for s in scratch],
        cost_estimate=pl.CostEstimate(flops=flops, bytes_accessed=moved, transcendentals=0),
        compiler_params=pltpu.CompilerParams(vmem_limit_bytes=40 << 20),
    )


FACES = [(3 * XROW, 128)] * 4 + [(512, 128)] * 2
BLOCK = (ROWS, 128)


def exchange(faces):
    sides = (("gx", 0, False), ("gx", 1, False), ("gy", 0, False), ("gy", 1, False), ("ha", 0, True), ("ha", 1, True))
    arrived = []
    for face, (axis, offset, closed) in zip(faces, sides):
        count = lax.axis_size(axis)
        pairs = []
        for i in range(offset, count if closed else count - 1, 2):
            pairs += [(i, (i + 1) % count), ((i + 1) % count, i)]
        arrived.append(lax.ppermute(face, axis, pairs))
    return arrived


def drift_tables(blocks):
    angle = np.arange(blocks * CH) * (2.0 * np.pi / (blocks * CH))
    speeds = 0.5 + np.arange(NV) / (NV - 1)
    tables, signs = [], []
    for part in (np.cos(angle), np.sin(angle)):
        part = np.where(np.abs(part) < 1e-12, 0.0, part).reshape(blocks, CH)
        positive = (part >= 0).all(axis=1)
        assert (positive | (part <= 0).all(axis=1)).all()
        tables.append(np.abs(part[:, :, None] * speeds).reshape(blocks, PAIRS, 2 * NV).astype(np.float32))
        signs.append(np.where(positive, 1, -1))
    return tables, signs


def steps(initial_value, request):
    tables, signs = drift_tables(lax.axis_size("ha"))
    ha = lax.axis_index("ha")
    adx, ady = (jnp.asarray(t)[ha] for t in tables)
    value, *faces = call(functools.partial(first_kernel, signs), "first", [BLOCK] + FACES, [VMEM])(initial_value)
    for step in range(STEPS):
        last = step == STEPS - 1
        arrived = exchange(faces)
        if step < 3:
            request = lax.all_to_all(request, ALL[step], split_axis=step, concat_axis=step, tiled=True)
        part, turned = call(
            functools.partial(inner_kernel, signs), "inner", [BLOCK] * 2, [VMEM] * 3, flops=30_000_000
        )(value, adx, ady)
        if step < 3:
            request, ady = lax.optimization_barrier((request, ady))
        value, *faces = call(
            functools.partial(outer_kernel, signs, last),
            "outer",
            [BLOCK] + ([initial_value.shape] if last else FACES),
            [VMEM] * 11,
            scratch=[(6 * XROW, 128), (6 * XROW, 128), (1024, 128), (1024, 128), BLOCK],
            flops=15_000_000,
        )(value, part, turned, adx, ady, *arrived)
    return value, faces[0], request


def sample_kernel(rows_ref, v_ref, at_ref, w_ref, out_ref, table, picked):
    first_half = lanes_first_half()

    def fill(n, _):
        tiles = [tile(v_ref, n * 256 + 8 * u) for u in range(32)]
        turned = [pltpu.roll(t, NV, 1) for t in tiles]
        for u in range(32):
            between = jnp.where(first_half, turned[u], pltpu.roll(turned[u], 7, 0))
            table[pl.ds(n * 512 + u * 16, 8, stride=2), :] = tiles[u]
            table[pl.ds(n * 512 + u * 16 + 1, 8, stride=2), :] = between
        return 0

    lax.fori_loop(0, 8, fill, 0)

    def pick(n, _):
        for u in range(8):
            s = n * 8 + u
            for j in range(4):
                row = rows_ref[s * 4 + j]
                for q, shift in enumerate((0, CH, CY * CH, CY * CH + CH)):
                    picked[pl.ds((q * 4 + j) * 256 + s, 1), :] = table[pl.ds(row + shift, 1), :]
        return 0

    lax.fori_loop(0, 32, pick, 0)
    lane = lax.broadcasted_iota(jnp.int32, (8, 128), 1)
    masks = [[((lane & 3) == j) & ((lane >> 4) == q) for q in range(4)] for j in range(4)]

    def weigh(n, _):
        for u in range(8):
            group = n * 8 + u
            total = jnp.zeros((8, 128), F32)
            for j in range(4):
                at = tile(at_ref, j * 256 + group * 8)
                for q in range(4):
                    read = jnp.take_along_axis(tile(picked, (q * 4 + j) * 256 + group * 8), at, axis=1)
                    total = jnp.where(masks[j][q], read, total)
            put(table, group * 8, total * tile(w_ref, group * 8))
        return 0

    lax.fori_loop(0, 4, weigh, 0)
    spread = lax.broadcasted_iota(jnp.int32, (128, 128), 0)
    slot = lax.broadcasted_iota(jnp.int32, (128, 128), 1)
    adder = ((spread < 64) & ((spread & 3) == slot)).astype(F32)
    sums = jnp.dot(
        table[pl.ds(0, 256), :], adder, precision=lax.Precision.HIGHEST, preferred_element_type=F32
    )
    out_ref[...] = sums[:, :4]


def local(initial_value, corner, weights):
    slots = corner.shape[1]
    owners = corner.shape[2]
    sizes = [lax.axis_size(a) for a in ALL]
    request = jnp.concatenate(
        [weights.reshape(16 * slots, owners), corner.reshape(slots, owners).astype(F32)], axis=0
    )
    request = jnp.pad(request.T, ((0, 0), (0, 128 - 17 * slots))).reshape(*sizes, 128)
    value, final, request = steps(initial_value, request)
    request = request.reshape(owners, 128)
    codes = jnp.maximum(request[:, 64 : 64 + slots], 0.0).astype(jnp.int32)
    lane = jnp.arange(128, dtype=jnp.int32)
    reads = (codes.T % NV)[:, :, None] + (((lane >> 2) & 1) + NV * ((lane >> 3) & 1))[None, None, :]
    (sums,) = call(
        sample_kernel,
        "samples",
        [(owners, slots)],
        [SMEM, VMEM, VMEM, VMEM],
        scratch=[(2 * ROWS, 128), (16 * owners, 128)],
    )(codes.reshape(-1) // NV, value, reads.reshape(slots * owners, 128), request)
    sampled = lax.all_to_all(sums, ALL, split_axis=0, concat_axis=0, tiled=True)
    sampled = jnp.where(corner >= 0, sampled.T.reshape(corner.shape), 0.0)
    return final, sampled


def solution(mesh):
    return jax.shard_map(
        local,
        mesh=mesh,
        in_specs=(
            P("gx", "gy", "ha"),
            P(("gx", "gy", "ha"), None, None),
            P(("gx", "gy", "ha"), None, None, None),
        ),
        out_specs=(P("gx", "gy", "ha"), P(("gx", "gy", "ha"), None, None)),
        check_vma=False,
    )
```

```python
import functools

import jax
import jax.numpy as jnp
import numpy as np
from jax import lax
from jax.experimental import pallas as pl
from jax.experimental.pallas import tpu as pltpu
from jax.sharding import PartitionSpec as P

NV = 64
STEPS = 4
EPS = 1e-06
DT = 0.15
CX = CY = CH = 16
PAIRS = CH // 2
ROWS = CX * CY * PAIRS
XROW = CY * PAIRS
YROW = PAIRS
F32 = jnp.float32
VMEM = pl.BlockSpec(memory_space=pltpu.VMEM)
SMEM = pl.BlockSpec(memory_space=pltpu.SMEM)
ALL = ("gx", "gy", "ha")

def smooth(low, high, turn):
    mid = (turn * (4.0 / 3.0)) * turn + low * high + EPS
    twice = turn + turn
    return mid + high * twice, mid, mid - low * twice


def inverse(d):
    r = pl.reciprocal(d, approx=True)
    return r * (2.0 - d * r)


def upwind(cells):
    count = len(cells) - 5
    diff = [cells[n + 1] - cells[n] for n in range(count + 4)]
    curve = [diff[n + 1] - diff[n] for n in range(count + 3)]
    turn = [curve[n + 1] - curve[n] for n in range(count + 2)]
    bend = [turn[n] - turn[n + 1] for n in range(count + 1)]
    terms = [smooth(curve[n], curve[n + 1], turn[n]) for n in range(count + 2)]
    slopes = []
    for n in range(count):
        a, b, c = terms[n][0], terms[n + 1][1], terms[n + 2][2]
        bc, ac, ab = b * c, a * c, a * b
        alpha, beta, gamma = bc * bc, ac * ac, ab * ab
        gamma3 = 3.0 * gamma
        down = alpha + 6.0 * beta + gamma3
        up = alpha * (bend[n] + bend[n]) + gamma3 * bend[n + 1]
        inner = curve[n + 1] + (curve[n + 2] + curve[n + 2]) + up * inverse(down)
        slopes.append(diff[n + 2] + inner * (1.0 / 6.0))
    return slopes


def heading_terms(pairs, turned, first_half):
    count = len(pairs)
    between = [jnp.where(first_half, turned[n], turned[n + 1]) for n in range(count - 1)]
    diff_e = [between[n] - pairs[n] for n in range(count - 1)]
    diff_o = [pairs[n + 1] - between[n] for n in range(count - 1)]
    curve_e = [diff_o[n] - diff_e[n] for n in range(count - 1)]
    curve_o = [diff_e[n + 1] - diff_o[n] for n in range(count - 2)]
    turn_e = [curve_o[n] - curve_e[n] for n in range(count - 2)]
    turn_o = [curve_e[n + 1] - curve_o[n] for n in range(count - 2)]
    even = [smooth(curve_e[n], curve_o[n], turn_e[n]) for n in range(count - 2)]
    odd = [smooth(curve_o[n], curve_e[n + 1], turn_o[n]) for n in range(count - 2)]

    def inner_sum(a, b, c, before, here, bend_a, bend_c):
        bc, ac, ab = b * c, a * c, a * b
        alpha, beta, gamma = bc * bc, ac * ac, ab * ab
        gamma3 = 3.0 * gamma
        down = alpha + 6.0 * beta + gamma3
        up = alpha * (bend_a + bend_a) + gamma3 * bend_c
        return before + (here + here) + up * inverse(down)

    result = []
    for n in range(2, count - 2):
        bend_m, bend_0, bend_p = (
            turn_o[n - 2] - turn_e[n - 1],
            turn_e[n - 1] - turn_o[n - 1],
            turn_o[n - 1] - turn_e[n],
        )
        minus = inner_sum(
            odd[n - 2][0], even[n - 1][1], odd[n - 1][2], curve_e[n - 1], curve_o[n - 1], bend_m, bend_0
        )
        plus = inner_sum(
            even[n][2], odd[n - 1][1], even[n - 1][0], curve_e[n], curve_o[n - 1], bend_p, bend_0
        )
        sixth = 1.0 / 6.0
        result.append(jnp.minimum(diff_o[n - 1] + minus * sixth, plus * sixth - diff_e[n]))
    return result


def tile(ref, row):
    return ref[pl.ds(pl.multiple_of(row, 8), 8), :]


def put(ref, row, value):
    ref[pl.ds(pl.multiple_of(row, 8), 8), :] = value


def lanes_first_half():
    return lax.broadcasted_iota(jnp.int32, (8, 128), 1) < NV


def scalars(signs):
    ha = lax.axis_index("ha")
    found = []
    for axis, sign in (("gx", signs[0]), ("gy", signs[1])):
        even = lax.rem(lax.axis_index(axis), 2) == 0
        wind = jnp.int32(int(sign[0]))
        for block in range(1, len(sign)):
            wind = jnp.where(ha == block, jnp.int32(int(sign[block])), wind)
        ahead = wind > 0
        high, low = jnp.where(ahead, 3, 2), jnp.where(ahead, 0, 5)
        found.append(
            (
                jnp.where(ahead, 0, 15),
                wind,
                jnp.where(even, 13, 0),
                jnp.where(even, 0, 13),
                jnp.where(even, high, low),
                jnp.where(even, low, high),
            )
        )
    even = lax.rem(ha, 2) == 0
    found.append(
        (jnp.where(even, 6, 0), jnp.where(even, 0, 6), jnp.where(even, 2, 0), jnp.where(even, 0, 2))
    )
    return found


def write_faces(where, v_ref, faces):
    (_, _, fx_a, fx_b, _, _), (_, _, fy_a, fy_b, _, _), (fh_a, fh_b, _, _) = where
    fxa, fxb, fya, fyb, fha, fhb = faces

    def body(n, _):
        for l in range(3):
            put(fxa, l * XROW + n * YROW, tile(v_ref, (fx_a + l) * XROW + n * YROW))
            put(fxb, l * XROW + n * YROW, tile(v_ref, (fx_b + l) * XROW + n * YROW))
            put(fya, l * XROW + n * YROW, tile(v_ref, n * XROW + (fy_a + l) * YROW))
            put(fyb, l * XROW + n * YROW, tile(v_ref, n * XROW + (fy_b + l) * YROW))
        for l in range(2):
            for t in range(2):
                base = n * XROW + t * 64
                out = (l * 32 + n * 2 + t) * 8
                put(fha, out, v_ref[pl.ds(base + fh_a + l, 8, stride=8), :])
                put(fhb, out, v_ref[pl.ds(base + fh_b + l, 8, stride=8), :])
        return 0

    lax.fori_loop(0, 16, body, 0, unroll=2)


def native(x, t, p):
    return x, pl.ds(8 * t, 8), pl.ds(128 * p, 128)


def first_kernel(signs, in_ref, _, v_ref, *faces):
    def body(x, _):
        for t in range(2):
            for p in range(8):
                v_ref[pl.ds(x * XROW + t * 64 + p, 8, stride=8), :] = in_ref[native(x, t, p)]
        return 0

    lax.fori_loop(0, 16, body, 0)
    write_faces(scalars(signs), v_ref, faces)


def inner_kernel(signs, v_ref, adx_ref, ady_ref, h_ref, turned_ref):
    (x_start, x_dir, *_), (y_start, y_dir, *_), _ = scalars(signs)
    first_half = lanes_first_half()
    adx, ady = adx_ref[...], ady_ref[...]
    zero = jnp.zeros((8, 128), F32)
    turned_ref[...] = pltpu.roll(v_ref[...], NV, 1)
    xs = [(x_start + x_dir * i) * XROW for i in range(16)]
    ys = [(y_start + y_dir * i) * YROW for i in range(16)]

    def along_x(y, _):
        slopes = upwind([tile(v_ref, row + y * YROW) for row in xs])
        for i in range(16):
            put(h_ref, xs[i] + y * YROW, adx * slopes[i - 3] if 3 <= i <= 13 else zero)
        return 0

    lax.fori_loop(0, 16, along_x, 0)

    def along_y(x, _):
        slopes = upwind([tile(v_ref, row + x * XROW) for row in ys])
        for i in range(3, 14):
            row = ys[i] + x * XROW
            put(h_ref, row, tile(h_ref, row) + ady * slopes[i - 3])
        return 0

    lax.fori_loop(0, 16, along_y, 0)

    def along_h(n, _):
        at = [pl.ds(n * 64 + p, 8, stride=8) for p in range(8)]
        terms = heading_terms([v_ref[a, :] for a in at], [turned_ref[a, :] for a in at], first_half)
        for a, term in zip(at[2:6], terms):
            h_ref[a, :] = h_ref[a, :] + term
        return 0

    lax.fori_loop(0, 32, along_h, 0)


def outer_kernel(
    signs, last, v_ref, h_in, turned_ref, adx_ref, ady_ref, rxa, rxb, rya, ryb, rha, rhb, *rest
):
    out_ref, others = rest[0], rest[1:-5]
    xs, ys, hs, hs_turned, h_ref = rest[-5:]
    where = scalars(signs)
    (x_start, x_dir, _, _, xh_a, xh_b), (y_start, y_dir, _, _, yh_a, yh_b), (_, _, hh_a, hh_b) = where
    first_half = lanes_first_half()
    adx, ady = adx_ref[...], ady_ref[...]
    for l in range(2):
        hs[pl.ds(pl.multiple_of((hh_a + l) * 256, 256), 256), :] = rha[pl.ds(l * 256, 256), :]
        hs[pl.ds(pl.multiple_of((hh_b + l) * 256, 256), 256), :] = rhb[pl.ds(l * 256, 256), :]
    hs_turned[...] = pltpu.roll(hs[...], NV, 1)
    for l in range(3):
        part = pl.ds(l * XROW, XROW)
        for ref, got, base, step in (
            (xs, rxa, xh_a, x_dir),
            (xs, rxb, xh_b, x_dir),
            (ys, rya, yh_a, y_dir),
            (ys, ryb, yh_b, y_dir),
        ):
            ref[pl.ds(pl.multiple_of((base + step * l) * XROW, XROW), XROW), :] = got[part, :]
    x_rows = [(x_start + x_dir * i) * XROW for i in range(16)]
    y_rows = [(y_start + y_dir * i) * YROW for i in range(16)]

    def edges(halo, at, rows, offset):
        own = {i: tile(v_ref, rows[i] + offset) for i in (0, 1, 2, 3, 4, 11, 12, 13, 14, 15)}
        ring = [tile(halo, l * XROW + at) for l in range(5)]
        low = upwind(ring[:3] + [own[i] for i in range(5)])
        high = upwind([own[i] for i in range(11, 16)] + ring[3:])
        return list(zip(range(3), low)) + list(zip(range(14, 16), high))

    def along_x(y, _):
        at = y * YROW
        for i, slope in edges(xs, at, x_rows, at):
            put(h_ref, x_rows[i] + at, tile(h_in, x_rows[i] + at) + adx * slope)
        for i in range(3, 14):
            put(h_ref, x_rows[i] + at, tile(h_in, x_rows[i] + at))
        return 0

    lax.fori_loop(0, 16, along_x, 0)

    def along_y(x, _):
        for i, slope in edges(ys, x * YROW, y_rows, x * XROW):
            row = y_rows[i] + x * XROW
            put(h_ref, row, tile(h_ref, row) + ady * slope)
        return 0

    lax.fori_loop(0, 16, along_y, 0)

    def along_h(n, _):
        at = [pl.ds(n * 64 + p, 8, stride=8) for p in range(8)]
        own = [v_ref[a, :] for a in at]
        own_turned = [turned_ref[a, :] for a in at]
        ring = [tile(hs, l * 256 + n * 8) for l in range(4)]
        ring_turned = [tile(hs_turned, l * 256 + n * 8) for l in range(4)]
        low = heading_terms(ring[:2] + own[:4], ring_turned[:2] + own_turned[:4], first_half)
        high = heading_terms(own[4:] + ring[2:], own_turned[4:] + ring_turned[2:], first_half)
        for p in range(8):
            total = h_ref[at[p], :]
            if p < 2:
                total = total + low[p]
            if p > 5:
                total = total + high[p - 6]
            value = own[p] - DT * jnp.maximum(total, 0.0)
            out_ref[at[p], :] = value
            if last:
                others[0][native(n // 2, lax.rem(n, 2), p)] = value
        return 0

    lax.fori_loop(0, 32, along_h, 0)
    if not last:
        write_faces(where, out_ref, others)


def call(body, name, outs, in_specs, scratch=(), flops=0, moved=4 << 20):
    return pl.pallas_call(
        body,
        name=name,
        out_shape=[jax.ShapeDtypeStruct(s, F32) for s in outs],
        in_specs=in_specs,
        out_specs=[VMEM] * len(outs),
        scratch_shapes=[pltpu.VMEM(s, F32) for s in scratch],
        cost_estimate=pl.CostEstimate(flops=flops, bytes_accessed=moved, transcendentals=0),
        compiler_params=pltpu.CompilerParams(vmem_limit_bytes=16 << 20),
    )


FACES = [(3 * XROW, 128)] * 4 + [(512, 128)] * 2
BLOCK = (ROWS, 128)


def exchange(faces):
    sides = (("gx", 0, False), ("gx", 1, False), ("gy", 0, False), ("gy", 1, False), ("ha", 0, True), ("ha", 1, True))
    arrived = []
    for face, (axis, offset, closed) in zip(faces, sides):
        count = lax.axis_size(axis)
        pairs = []
        for i in range(offset, count if closed else count - 1, 2):
            pairs += [(i, (i + 1) % count), ((i + 1) % count, i)]
        arrived.append(lax.ppermute(face, axis, pairs))
    return arrived


def drift_tables(blocks):
    angle = np.arange(blocks * CH) * (2.0 * np.pi / (blocks * CH))
    speeds = 0.5 + np.arange(NV) / (NV - 1)
    tables, signs = [], []
    for part in (np.cos(angle), np.sin(angle)):
        part = np.where(np.abs(part) < 1e-12, 0.0, part).reshape(blocks, CH)
        positive = (part >= 0).all(axis=1)
        assert (positive | (part <= 0).all(axis=1)).all()
        tables.append(np.abs(part[:, :, None] * speeds).reshape(blocks, PAIRS, 2 * NV).astype(np.float32))
        signs.append(np.where(positive, 1, -1))
    return tables, signs


def steps(initial_value, request):
    tables, signs = drift_tables(lax.axis_size("ha"))
    ha = lax.axis_index("ha")
    adx, ady = (jnp.asarray(t)[ha] for t in tables)
    request = lax.all_to_all(request, ALL, split_axis=0, concat_axis=0, tiled=True)
    value, *faces = call(
        functools.partial(first_kernel, signs), "first", [BLOCK] + FACES, [VMEM, pl.BlockSpec(memory_space=pl.ANY)]
    )(initial_value, request)
    for step in range(STEPS):
        last = step == STEPS - 1
        arrived = exchange(faces)
        part, turned = call(
            functools.partial(inner_kernel, signs), "inner", [BLOCK] * 2, [VMEM] * 3, flops=30_000_000
        )(value, adx, ady)
        value, *faces = call(
            functools.partial(outer_kernel, signs, last),
            "outer",
            [BLOCK] + ([initial_value.shape] if last else FACES),
            [VMEM] * 11,
            scratch=[(6 * XROW, 128), (6 * XROW, 128), (1024, 128), (1024, 128), BLOCK],
            flops=15_000_000,
        )(value, part, turned, adx, ady, *arrived)
    return value, faces[0], request


def sample_kernel(rows_ref, v_ref, at_ref, w_ref, out_ref, table, picked):
    first_half = lanes_first_half()

    def fill(n, _):
        tiles = [tile(v_ref, n * 256 + 8 * u) for u in range(32)]
        turned = [pltpu.roll(t, NV, 1) for t in tiles]
        for u in range(32):
            between = jnp.where(first_half, turned[u], pltpu.roll(turned[u], 7, 0))
            table[pl.ds(n * 512 + u * 16, 8, stride=2), :] = tiles[u]
            table[pl.ds(n * 512 + u * 16 + 1, 8, stride=2), :] = between
        return 0

    lax.fori_loop(0, 8, fill, 0)

    def pick(n, _):
        for u in range(8):
            s = n * 8 + u
            for j in range(4):
                row = rows_ref[s * 4 + j]
                for q, shift in enumerate((0, CH, CY * CH, CY * CH + CH)):
                    picked[pl.ds((q * 4 + j) * 256 + s, 1), :] = table[pl.ds(row + shift, 1), :]
        return 0

    lax.fori_loop(0, 32, pick, 0)
    lane = lax.broadcasted_iota(jnp.int32, (8, 128), 1)
    masks = [[((lane & 3) == j) & ((lane >> 4) == q) for q in range(4)] for j in range(4)]

    def weigh(n, _):
        for u in range(8):
            group = n * 8 + u
            total = jnp.zeros((8, 128), F32)
            for j in range(4):
                at = tile(at_ref, j * 256 + group * 8)
                for q in range(4):
                    read = jnp.take_along_axis(tile(picked, (q * 4 + j) * 256 + group * 8), at, axis=1)
                    total = jnp.where(masks[j][q], read, total)
            put(table, group * 8, total * tile(w_ref, group * 8))
        return 0

    lax.fori_loop(0, 4, weigh, 0)
    spread = lax.broadcasted_iota(jnp.int32, (128, 128), 0)
    slot = lax.broadcasted_iota(jnp.int32, (128, 128), 1)
    adder = ((spread < 64) & ((spread & 3) == slot)).astype(F32)
    sums = jnp.dot(
        table[pl.ds(0, 256), :], adder, precision=lax.Precision.HIGHEST, preferred_element_type=F32
    )
    out_ref[...] = sums[:, :4]


def local(initial_value, corner, weights):
    slots = corner.shape[1]
    owners = corner.shape[2]
    request = jnp.concatenate(
        [weights.reshape(16 * slots, owners), corner.reshape(slots, owners).astype(F32)], axis=0
    )
    request = jnp.pad(request.T, ((0, 0), (0, 128 - 17 * slots)))
    value, final, request = steps(initial_value, request)
    codes = jnp.maximum(request[:, 64 : 64 + slots], 0.0).astype(jnp.int32)
    lane = jnp.arange(128, dtype=jnp.int32)
    reads = (codes.T % NV)[:, :, None] + (((lane >> 2) & 1) + NV * ((lane >> 3) & 1))[None, None, :]
    (sums,) = call(
        sample_kernel,
        "samples",
        [(owners, slots)],
        [SMEM, VMEM, VMEM, VMEM],
        scratch=[(2 * ROWS, 128), (16 * owners, 128)],
    )(codes.reshape(-1) // NV, value, reads.reshape(slots * owners, 128), request)
    sampled = lax.all_to_all(sums, ALL, split_axis=0, concat_axis=0, tiled=True)
    sampled = jnp.where(corner >= 0, sampled.T.reshape(corner.shape), 0.0)
    return final, sampled


def solution(mesh):
    return jax.shard_map(
        local,
        mesh=mesh,
        in_specs=(
            P("gx", "gy", "ha"),
            P(("gx", "gy", "ha"), None, None),
            P(("gx", "gy", "ha"), None, None, None),
        ),
        out_specs=(P("gx", "gy", "ha"), P(("gx", "gy", "ha"), None, None)),
        check_vma=False,
    )
```

```python
import functools

import jax
import jax.numpy as jnp
import numpy as np
from jax import lax
from jax.experimental import pallas as pl
from jax.experimental.pallas import tpu as pltpu
from jax.sharding import PartitionSpec as P

NV = 64
STEPS = 4
EPS = 1e-06
DT = 0.15
CX = CY = CH = 16
PAIRS = CH // 2
ROWS = CX * CY * PAIRS
XROW = CY * PAIRS
YROW = PAIRS
F32 = jnp.float32
VMEM = pl.BlockSpec(memory_space=pltpu.VMEM)
ANY = pl.BlockSpec(memory_space=pl.ANY)
SMEM = pl.BlockSpec(memory_space=pltpu.SMEM)
ALL = ("gx", "gy", "ha")

def smooth(low, high, low2, high2, turn):
    mid = (turn * (4.0 / 3.0)) * turn + low * high + EPS
    return mid + high2 * turn, mid, mid - low2 * turn


def inverse(d):
    r = pl.reciprocal(d, approx=True)
    return r * (2.0 - d * r)


def upwind(cells):
    count = len(cells) - 5
    diff = [cells[n + 1] - cells[n] for n in range(count + 4)]
    curve = [diff[n + 1] - diff[n] for n in range(count + 3)]
    turn = [curve[n + 1] - curve[n] for n in range(count + 2)]
    bend = [turn[n] - turn[n + 1] for n in range(count + 1)]
    curve2 = [c + c for c in curve]
    terms = [smooth(curve[n], curve[n + 1], curve2[n], curve2[n + 1], turn[n]) for n in range(count + 2)]
    slopes = []
    for n in range(count):
        a, b, c = terms[n][0], terms[n + 1][1], terms[n + 2][2]
        bc, ac, ab = b * c, a * c, a * b
        alpha, beta, gamma = bc * bc, ac * ac, ab * ab
        gamma3 = 3.0 * gamma
        down = alpha + 6.0 * beta + gamma3
        up = alpha * (bend[n] + bend[n]) + gamma3 * bend[n + 1]
        inner = curve[n + 1] + curve2[n + 2] + up * inverse(down)
        slopes.append(diff[n + 2] + inner * (1.0 / 6.0))
    return slopes


def heading_terms(pairs, turned, first_half):
    count = len(pairs)
    between = [jnp.where(first_half, turned[n], turned[n + 1]) for n in range(count - 1)]
    diff_e = [between[n] - pairs[n] for n in range(count - 1)]
    diff_o = [pairs[n + 1] - between[n] for n in range(count - 1)]
    curve_e = [diff_o[n] - diff_e[n] for n in range(count - 1)]
    curve_o = [diff_e[n + 1] - diff_o[n] for n in range(count - 2)]
    turn_e = [curve_o[n] - curve_e[n] for n in range(count - 2)]
    turn_o = [curve_e[n + 1] - curve_o[n] for n in range(count - 2)]
    two_e, two_o = [c + c for c in curve_e], [c + c for c in curve_o]
    even = [smooth(curve_e[n], curve_o[n], two_e[n], two_o[n], turn_e[n]) for n in range(count - 2)]
    odd = [
        smooth(curve_o[n], curve_e[n + 1], two_o[n], two_e[n + 1], turn_o[n]) for n in range(count - 2)
    ]

    def inner_sum(a, b, c, before, here2, bend_a, bend_c):
        bc, ac, ab = b * c, a * c, a * b
        alpha, beta, gamma = bc * bc, ac * ac, ab * ab
        gamma3 = 3.0 * gamma
        down = alpha + 6.0 * beta + gamma3
        up = alpha * (bend_a + bend_a) + gamma3 * bend_c
        return before + here2 + up * inverse(down)

    result = []
    for n in range(2, count - 2):
        bend_m, bend_0, bend_p = (
            turn_o[n - 2] - turn_e[n - 1],
            turn_e[n - 1] - turn_o[n - 1],
            turn_o[n - 1] - turn_e[n],
        )
        minus = inner_sum(
            odd[n - 2][0], even[n - 1][1], odd[n - 1][2], curve_e[n - 1], two_o[n - 1], bend_m, bend_0
        )
        plus = inner_sum(
            even[n][2], odd[n - 1][1], even[n - 1][0], curve_e[n], two_o[n - 1], bend_p, bend_0
        )
        sixth = 1.0 / 6.0
        result.append(jnp.minimum(diff_o[n - 1] + minus * sixth, plus * sixth - diff_e[n]))
    return result


def tile(ref, row):
    return ref[pl.ds(pl.multiple_of(row, 8), 8), :]


def put(ref, row, value):
    ref[pl.ds(pl.multiple_of(row, 8), 8), :] = value


def lanes_first_half():
    return lax.broadcasted_iota(jnp.int32, (8, 128), 1) < NV


def scalars(signs):
    ha = lax.axis_index("ha")
    found = []
    for axis, sign in (("gx", signs[0]), ("gy", signs[1])):
        even = lax.rem(lax.axis_index(axis), 2) == 0
        wind = jnp.int32(int(sign[0]))
        for block in range(1, len(sign)):
            wind = jnp.where(ha == block, jnp.int32(int(sign[block])), wind)
        ahead = wind > 0
        high, low = jnp.where(ahead, 3, 2), jnp.where(ahead, 0, 5)
        found.append(
            (
                jnp.where(ahead, 0, 15),
                wind,
                jnp.where(even, 13, 0),
                jnp.where(even, 0, 13),
                jnp.where(even, high, low),
                jnp.where(even, low, high),
            )
        )
    even = lax.rem(ha, 2) == 0
    found.append(
        (jnp.where(even, 6, 0), jnp.where(even, 0, 6), jnp.where(even, 2, 0), jnp.where(even, 0, 2))
    )
    return found


def write_faces(where, v_ref, faces):
    (_, _, fx_a, fx_b, _, _), (_, _, fy_a, fy_b, _, _), (fh_a, fh_b, _, _) = where
    fxa, fxb, fya, fyb, fha, fhb = faces

    def body(n, _):
        for l in range(3):
            put(fxa, l * XROW + n * YROW, tile(v_ref, (fx_a + l) * XROW + n * YROW))
            put(fxb, l * XROW + n * YROW, tile(v_ref, (fx_b + l) * XROW + n * YROW))
            put(fya, l * XROW + n * YROW, tile(v_ref, n * XROW + (fy_a + l) * YROW))
            put(fyb, l * XROW + n * YROW, tile(v_ref, n * XROW + (fy_b + l) * YROW))
        for l in range(2):
            for t in range(2):
                base = n * XROW + t * 64
                out = (l * 32 + n * 2 + t) * 8
                put(fha, out, v_ref[pl.ds(base + fh_a + l, 8, stride=8), :])
                put(fhb, out, v_ref[pl.ds(base + fh_b + l, 8, stride=8), :])
        return 0

    lax.fori_loop(0, 16, body, 0, unroll=2)


def native(x, t, p):
    return x, pl.ds(8 * t, 8), pl.ds(128 * p, 128)


def first_kernel(signs, in_ref, rows_ref, reads_ref, v_ref, *faces):
    def body(x, _):
        for t in range(2):
            for p in range(8):
                v_ref[pl.ds(x * XROW + t * 64 + p, 8, stride=8), :] = in_ref[native(x, t, p)]
        return 0

    lax.fori_loop(0, 16, body, 0)
    write_faces(scalars(signs), v_ref, faces)


def inner_kernel(signs, v_ref, adx_ref, ady_ref, h_ref, turned_ref):
    (x_start, x_dir, *_), (y_start, y_dir, *_), _ = scalars(signs)
    first_half = lanes_first_half()
    adx, ady = adx_ref[lax.axis_index("ha")], ady_ref[lax.axis_index("ha")]
    zero = jnp.zeros((8, 128), F32)
    turned_ref[...] = pltpu.roll(v_ref[...], NV, 1)
    xs = [(x_start + x_dir * i) * XROW for i in range(16)]
    ys = [(y_start + y_dir * i) * YROW for i in range(16)]

    def along_x(y, _):
        slopes = upwind([tile(v_ref, row + y * YROW) for row in xs])
        for i in range(16):
            put(h_ref, xs[i] + y * YROW, adx * slopes[i - 3] if 3 <= i <= 13 else zero)
        return 0

    lax.fori_loop(0, 16, along_x, 0)

    def along_y(x, _):
        slopes = upwind([tile(v_ref, row + x * XROW) for row in ys])
        for i in range(3, 14):
            row = ys[i] + x * XROW
            put(h_ref, row, tile(h_ref, row) + ady * slopes[i - 3])
        return 0

    lax.fori_loop(0, 16, along_y, 0)

    def along_h(n, _):
        at = [pl.ds(n * 64 + p, 8, stride=8) for p in range(8)]
        terms = heading_terms([v_ref[a, :] for a in at], [turned_ref[a, :] for a in at], first_half)
        for a, term in zip(at[2:6], terms):
            h_ref[a, :] = h_ref[a, :] + term
        return 0

    lax.fori_loop(0, 32, along_h, 0)


def outer_kernel(
    signs, last, v_ref, h_in, turned_ref, adx_ref, ady_ref, rxa, rxb, rya, ryb, rha, rhb, *rest
):
    out_ref, others = rest[0], rest[1:-5]
    xs, ys, hs, hs_turned, h_ref = rest[-5:]
    where = scalars(signs)
    (x_start, x_dir, _, _, xh_a, xh_b), (y_start, y_dir, _, _, yh_a, yh_b), (_, _, hh_a, hh_b) = where
    first_half = lanes_first_half()
    adx, ady = adx_ref[lax.axis_index("ha")], ady_ref[lax.axis_index("ha")]
    for l in range(2):
        hs[pl.ds(pl.multiple_of((hh_a + l) * 256, 256), 256), :] = rha[pl.ds(l * 256, 256), :]
        hs[pl.ds(pl.multiple_of((hh_b + l) * 256, 256), 256), :] = rhb[pl.ds(l * 256, 256), :]
    hs_turned[...] = pltpu.roll(hs[...], NV, 1)
    for l in range(3):
        part = pl.ds(l * XROW, XROW)
        for ref, got, base, step in (
            (xs, rxa, xh_a, x_dir),
            (xs, rxb, xh_b, x_dir),
            (ys, rya, yh_a, y_dir),
            (ys, ryb, yh_b, y_dir),
        ):
            ref[pl.ds(pl.multiple_of((base + step * l) * XROW, XROW), XROW), :] = got[part, :]
    x_rows = [(x_start + x_dir * i) * XROW for i in range(16)]
    y_rows = [(y_start + y_dir * i) * YROW for i in range(16)]

    def edges(halo, at, rows, offset):
        own = {i: tile(v_ref, rows[i] + offset) for i in (0, 1, 2, 3, 4, 11, 12, 13, 14, 15)}
        ring = [tile(halo, l * XROW + at) for l in range(5)]
        low = upwind(ring[:3] + [own[i] for i in range(5)])
        high = upwind([own[i] for i in range(11, 16)] + ring[3:])
        return list(zip(range(3), low)) + list(zip(range(14, 16), high))

    def along_x(y, _):
        at = y * YROW
        for i, slope in edges(xs, at, x_rows, at):
            put(h_ref, x_rows[i] + at, tile(h_in, x_rows[i] + at) + adx * slope)
        for i in range(3, 14):
            put(h_ref, x_rows[i] + at, tile(h_in, x_rows[i] + at))
        return 0

    lax.fori_loop(0, 16, along_x, 0)

    def along_y(x, _):
        for i, slope in edges(ys, x * YROW, y_rows, x * XROW):
            row = y_rows[i] + x * XROW
            put(h_ref, row, tile(h_ref, row) + ady * slope)
        return 0

    lax.fori_loop(0, 16, along_y, 0)

    def along_h(n, _):
        at = [pl.ds(n * 64 + p, 8, stride=8) for p in range(8)]
        own = [v_ref[a, :] for a in at]
        own_turned = [turned_ref[a, :] for a in at]
        ring = [tile(hs, l * 256 + n * 8) for l in range(4)]
        ring_turned = [tile(hs_turned, l * 256 + n * 8) for l in range(4)]
        low = heading_terms(ring[:2] + own[:4], ring_turned[:2] + own_turned[:4], first_half)
        high = heading_terms(own[4:] + ring[2:], own_turned[4:] + ring_turned[2:], first_half)
        for p in range(8):
            total = h_ref[at[p], :]
            if p < 2:
                total = total + low[p]
            if p > 5:
                total = total + high[p - 6]
            value = own[p] - DT * jnp.maximum(total, 0.0)
            out_ref[at[p], :] = value
            if last:
                others[0][native(n // 2, lax.rem(n, 2), p)] = value
        return 0

    lax.fori_loop(0, 32, along_h, 0)
    if not last:
        write_faces(where, out_ref, others)


def call(body, name, outs, in_specs, scratch=(), flops=0, moved=4 << 20):
    return pl.pallas_call(
        body,
        name=name,
        out_shape=[jax.ShapeDtypeStruct(s, F32) for s in outs],
        in_specs=in_specs,
        out_specs=[VMEM] * len(outs),
        scratch_shapes=[pltpu.VMEM(s, F32) for s in scratch],
        cost_estimate=pl.CostEstimate(flops=flops, bytes_accessed=moved, transcendentals=0),
        compiler_params=pltpu.CompilerParams(vmem_limit_bytes=8 << 20),
    )


FACES = [(3 * XROW, 128)] * 4 + [(512, 128)] * 2
BLOCK = (ROWS, 128)


def exchange(faces):
    sides = (("gx", 0, False), ("gx", 1, False), ("gy", 0, False), ("gy", 1, False), ("ha", 0, True), ("ha", 1, True))
    arrived = []
    for face, (axis, offset, closed) in zip(faces, sides):
        count = lax.axis_size(axis)
        pairs = []
        for i in range(offset, count if closed else count - 1, 2):
            pairs += [(i, (i + 1) % count), ((i + 1) % count, i)]
        arrived.append(lax.ppermute(face, axis, pairs))
    return arrived


def drift_tables(blocks):
    angle = np.arange(blocks * CH) * (2.0 * np.pi / (blocks * CH))
    speeds = 0.5 + np.arange(NV) / (NV - 1)
    tables, signs = [], []
    for part in (np.cos(angle), np.sin(angle)):
        part = np.where(np.abs(part) < 1e-12, 0.0, part).reshape(blocks, CH)
        positive = (part >= 0).all(axis=1)
        assert (positive | (part <= 0).all(axis=1)).all()
        tables.append(np.abs(part[:, :, None] * speeds).reshape(blocks, PAIRS, 2 * NV).astype(np.float32))
        signs.append(np.where(positive, 1, -1))
    return tables, signs


def steps(initial_value, rows, reads):
    tables, signs = drift_tables(lax.axis_size("ha"))
    adx, ady = (jnp.asarray(t) for t in tables)
    value, *faces = call(
        functools.partial(first_kernel, signs), "first", [BLOCK] + FACES, [VMEM, ANY, ANY]
    )(initial_value, rows, reads)
    for step in range(STEPS):
        last = step == STEPS - 1
        arrived = exchange(faces)
        part, turned = call(
            functools.partial(inner_kernel, signs), "inner", [BLOCK] * 2, [VMEM] * 3, flops=30_000_000
        )(value, adx, ady)
        value, *faces = call(
            functools.partial(outer_kernel, signs, last),
            "outer",
            [BLOCK] + ([initial_value.shape] if last else FACES),
            [VMEM] * 11,
            scratch=[(6 * XROW, 128), (6 * XROW, 128), (1024, 128), (1024, 128), BLOCK],
            flops=15_000_000,
        )(value, part, turned, adx, ady, *arrived)
    return value, faces[0]


def sample_kernel(rows_ref, v_ref, at_ref, w_ref, out_ref, table, picked):
    first_half = lanes_first_half()

    def fill(n, _):
        tiles = [tile(v_ref, n * 256 + 8 * u) for u in range(32)]
        turned = [pltpu.roll(t, NV, 1) for t in tiles]
        for u in range(32):
            between = jnp.where(first_half, turned[u], pltpu.roll(turned[u], 7, 0))
            table[pl.ds(n * 512 + u * 16, 8, stride=2), :] = tiles[u]
            table[pl.ds(n * 512 + u * 16 + 1, 8, stride=2), :] = between
        return 0

    lax.fori_loop(0, 8, fill, 0)

    def pick(n, _):
        for u in range(8):
            s = n * 8 + u
            for j in range(4):
                row = rows_ref[s * 4 + j]
                for q, shift in enumerate((0, CH, CY * CH, CY * CH + CH)):
                    picked[pl.ds((q * 4 + j) * 256 + s, 1), :] = table[pl.ds(row + shift, 1), :]
        return 0

    lax.fori_loop(0, 32, pick, 0)
    lane = lax.broadcasted_iota(jnp.int32, (8, 128), 1)
    masks = [[((lane & 3) == j) & ((lane >> 4) == q) for q in range(4)] for j in range(4)]

    def weigh(n, _):
        for u in range(8):
            group = n * 8 + u
            total = jnp.zeros((8, 128), F32)
            for j in range(4):
                at = tile(at_ref, j * 256 + group * 8)
                for q in range(4):
                    read = jnp.take_along_axis(tile(picked, (q * 4 + j) * 256 + group * 8), at, axis=1)
                    total = jnp.where(masks[j][q], read, total)
            put(table, group * 8, total * tile(w_ref, group * 8))
        return 0

    lax.fori_loop(0, 4, weigh, 0)
    spread = lax.broadcasted_iota(jnp.int32, (128, 128), 0)
    slot = lax.broadcasted_iota(jnp.int32, (128, 128), 1)
    adder = ((spread < 64) & ((spread & 3) == slot)).astype(F32)
    sums = jnp.dot(
        table[pl.ds(0, 256), :], adder, precision=lax.Precision.HIGHEST, preferred_element_type=F32
    )
    out_ref[...] = sums[:, :4]


def local(initial_value, corner, weights):
    slots = corner.shape[1]
    owners = corner.shape[2]
    request = jnp.concatenate(
        [weights.reshape(16 * slots, owners), corner.reshape(slots, owners).astype(F32)], axis=0
    )
    request = jnp.pad(request.T, ((0, 0), (0, 128 - 17 * slots)))
    request = lax.all_to_all(request, ALL, split_axis=0, concat_axis=0, tiled=True)
    codes = jnp.maximum(request[:, 64 : 64 + slots], 0.0).astype(jnp.int32)
    lane = jnp.arange(128, dtype=jnp.int32)
    reads = (codes.T % NV)[:, :, None] + (((lane >> 2) & 1) + NV * ((lane >> 3) & 1))[None, None, :]
    rows = codes.reshape(-1) // NV
    reads = reads.reshape(slots * owners, 128)
    value, final = steps(initial_value, rows, reads)
    (sums,) = call(
        sample_kernel,
        "samples",
        [(owners, slots)],
        [SMEM, VMEM, VMEM, VMEM],
        scratch=[(2 * ROWS, 128), (16 * owners, 128)],
    )(rows, value, reads, request)
    sampled = lax.all_to_all(sums, ALL, split_axis=0, concat_axis=0, tiled=True)
    sampled = jnp.where(corner >= 0, sampled.T.reshape(corner.shape), 0.0)
    return final, sampled


def solution(mesh):
    return jax.shard_map(
        local,
        mesh=mesh,
        in_specs=(
            P("gx", "gy", "ha"),
            P(("gx", "gy", "ha"), None, None),
            P(("gx", "gy", "ha"), None, None, None),
        ),
        out_specs=(P("gx", "gy", "ha"), P(("gx", "gy", "ha"), None, None)),
        check_vma=False,
    )
```

```python
import functools

import jax
import jax.numpy as jnp
import numpy as np
from jax import lax
from jax.experimental import pallas as pl
from jax.experimental.pallas import tpu as pltpu
from jax.sharding import PartitionSpec as P

NV = 64
STEPS = 4
EPS = 1e-06
DT = 0.15
CX = CY = CH = 16
PAIRS = CH // 2
ROWS = CX * CY * PAIRS
XROW = CY * PAIRS
YROW = PAIRS
F32 = jnp.float32
VMEM = pl.BlockSpec(memory_space=pltpu.VMEM)
ANY = pl.BlockSpec(memory_space=pl.ANY)
SMEM = pl.BlockSpec(memory_space=pltpu.SMEM)
ALL = ("gx", "gy", "ha")

def smooth(low, high, low2, high2, turn):
    mid = (turn * (4.0 / 3.0)) * turn + low * high + EPS
    return mid + high2 * turn, mid, mid - low2 * turn


def inverse(d):
    r = pl.reciprocal(d, approx=True)
    return r * (2.0 - d * r)


def upwind(cells):
    count = len(cells) - 5
    diff = [cells[n + 1] - cells[n] for n in range(count + 4)]
    curve = [diff[n + 1] - diff[n] for n in range(count + 3)]
    turn = [curve[n + 1] - curve[n] for n in range(count + 2)]
    bend = [turn[n] - turn[n + 1] for n in range(count + 1)]
    curve2 = [c + c for c in curve]
    terms = [smooth(curve[n], curve[n + 1], curve2[n], curve2[n + 1], turn[n]) for n in range(count + 2)]
    slopes = []
    for n in range(count):
        a, b, c = terms[n][0], terms[n + 1][1], terms[n + 2][2]
        bc, ac, ab = b * c, a * c, a * b
        alpha, beta, gamma = bc * bc, ac * ac, ab * ab
        gamma3 = 3.0 * gamma
        down = alpha + 6.0 * beta + gamma3
        up = alpha * (bend[n] + bend[n]) + gamma3 * bend[n + 1]
        inner = curve[n + 1] + curve2[n + 2] + up * inverse(down)
        slopes.append(diff[n + 2] + inner * (1.0 / 6.0))
    return slopes


def heading_terms(pairs, turned, first_half):
    count = len(pairs)
    between = [jnp.where(first_half, turned[n], turned[n + 1]) for n in range(count - 1)]
    diff_e = [between[n] - pairs[n] for n in range(count - 1)]
    diff_o = [pairs[n + 1] - between[n] for n in range(count - 1)]
    curve_e = [diff_o[n] - diff_e[n] for n in range(count - 1)]
    curve_o = [diff_e[n + 1] - diff_o[n] for n in range(count - 2)]
    turn_e = [curve_o[n] - curve_e[n] for n in range(count - 2)]
    turn_o = [curve_e[n + 1] - curve_o[n] for n in range(count - 2)]
    two_e, two_o = [c + c for c in curve_e], [c + c for c in curve_o]
    even = [smooth(curve_e[n], curve_o[n], two_e[n], two_o[n], turn_e[n]) for n in range(count - 2)]
    odd = [
        smooth(curve_o[n], curve_e[n + 1], two_o[n], two_e[n + 1], turn_o[n]) for n in range(count - 2)
    ]

    def inner_sum(a, b, c, before, here2, bend_a, bend_c):
        bc, ac, ab = b * c, a * c, a * b
        alpha, beta, gamma = bc * bc, ac * ac, ab * ab
        gamma3 = 3.0 * gamma
        down = alpha + 6.0 * beta + gamma3
        up = alpha * (bend_a + bend_a) + gamma3 * bend_c
        return before + here2 + up * inverse(down)

    result = []
    for n in range(2, count - 2):
        bend_m, bend_0, bend_p = (
            turn_o[n - 2] - turn_e[n - 1],
            turn_e[n - 1] - turn_o[n - 1],
            turn_o[n - 1] - turn_e[n],
        )
        minus = inner_sum(
            odd[n - 2][0], even[n - 1][1], odd[n - 1][2], curve_e[n - 1], two_o[n - 1], bend_m, bend_0
        )
        plus = inner_sum(
            even[n][2], odd[n - 1][1], even[n - 1][0], curve_e[n], two_o[n - 1], bend_p, bend_0
        )
        sixth = 1.0 / 6.0
        result.append(jnp.minimum(diff_o[n - 1] + minus * sixth, plus * sixth - diff_e[n]))
    return result


def tile(ref, row):
    return ref[pl.ds(pl.multiple_of(row, 8), 8), :]


def put(ref, row, value):
    ref[pl.ds(pl.multiple_of(row, 8), 8), :] = value


def lanes_first_half():
    return lax.broadcasted_iota(jnp.int32, (8, 128), 1) < NV


def scalars(signs):
    ha = lax.axis_index("ha")
    found = []
    for axis, sign in (("gx", signs[0]), ("gy", signs[1])):
        even = lax.rem(lax.axis_index(axis), 2) == 0
        wind = jnp.int32(int(sign[0]))
        for block in range(1, len(sign)):
            wind = jnp.where(ha == block, jnp.int32(int(sign[block])), wind)
        ahead = wind > 0
        high, low = jnp.where(ahead, 3, 2), jnp.where(ahead, 0, 5)
        found.append(
            (
                jnp.where(ahead, 0, 15),
                wind,
                jnp.where(even, 13, 0),
                jnp.where(even, 0, 13),
                jnp.where(even, high, low),
                jnp.where(even, low, high),
            )
        )
    even = lax.rem(ha, 2) == 0
    found.append(
        (jnp.where(even, 6, 0), jnp.where(even, 0, 6), jnp.where(even, 2, 0), jnp.where(even, 0, 2))
    )
    return found


def write_faces(where, v_ref, faces):
    (_, _, fx_a, fx_b, _, _), (_, _, fy_a, fy_b, _, _), (fh_a, fh_b, _, _) = where
    fxa, fxb, fya, fyb, fha, fhb = faces

    def body(n, _):
        for l in range(3):
            put(fxa, l * XROW + n * YROW, tile(v_ref, (fx_a + l) * XROW + n * YROW))
            put(fxb, l * XROW + n * YROW, tile(v_ref, (fx_b + l) * XROW + n * YROW))
            put(fya, l * XROW + n * YROW, tile(v_ref, n * XROW + (fy_a + l) * YROW))
            put(fyb, l * XROW + n * YROW, tile(v_ref, n * XROW + (fy_b + l) * YROW))
        for l in range(2):
            for t in range(2):
                base = n * XROW + t * 64
                out = (l * 32 + n * 2 + t) * 8
                put(fha, out, v_ref[pl.ds(base + fh_a + l, 8, stride=8), :])
                put(fhb, out, v_ref[pl.ds(base + fh_b + l, 8, stride=8), :])
        return 0

    lax.fori_loop(0, 16, body, 0, unroll=2)


def native(x, t, p):
    return x, pl.ds(8 * t, 8), pl.ds(128 * p, 128)


def first_kernel(signs, in_ref, rows_ref, reads_ref, v_ref, *faces):
    def body(x, _):
        for t in range(2):
            for p in range(8):
                v_ref[pl.ds(x * XROW + t * 64 + p, 8, stride=8), :] = in_ref[native(x, t, p)]
        return 0

    lax.fori_loop(0, 16, body, 0)
    write_faces(scalars(signs), v_ref, faces)


def inner_kernel(signs, v_ref, adx_ref, ady_ref, h_ref, turned_ref):
    (x_start, x_dir, *_), (y_start, y_dir, *_), _ = scalars(signs)
    first_half = lanes_first_half()
    adx, ady = adx_ref[lax.axis_index("ha")], ady_ref[lax.axis_index("ha")]
    zero = jnp.zeros((8, 128), F32)
    turned_ref[...] = pltpu.roll(v_ref[...], NV, 1)
    xs = [(x_start + x_dir * i) * XROW for i in range(16)]
    ys = [(y_start + y_dir * i) * YROW for i in range(16)]

    def along_x(y, _):
        slopes = upwind([tile(v_ref, row + y * YROW) for row in xs])
        for i in range(16):
            put(h_ref, xs[i] + y * YROW, adx * slopes[i - 3] if 3 <= i <= 13 else zero)
        return 0

    lax.fori_loop(0, 16, along_x, 0)

    def along_y(x, _):
        slopes = upwind([tile(v_ref, row + x * XROW) for row in ys])
        for i in range(3, 14):
            row = ys[i] + x * XROW
            put(h_ref, row, tile(h_ref, row) + ady * slopes[i - 3])
        return 0

    lax.fori_loop(0, 16, along_y, 0)

    def along_h(n, _):
        at = [pl.ds(n * 64 + p, 8, stride=8) for p in range(8)]
        terms = heading_terms([v_ref[a, :] for a in at], [turned_ref[a, :] for a in at], first_half)
        for a, term in zip(at[2:6], terms):
            h_ref[a, :] = h_ref[a, :] + term
        return 0

    lax.fori_loop(0, 32, along_h, 0)


def outer_kernel(
    signs, last, v_ref, h_in, turned_ref, adx_ref, ady_ref, rxa, rxb, rya, ryb, rha, rhb, *rest
):
    out_ref, others = rest[0], rest[1:-5]
    xs, ys, hs, hs_turned, h_ref = rest[-5:]
    where = scalars(signs)
    (x_start, x_dir, _, _, xh_a, xh_b), (y_start, y_dir, _, _, yh_a, yh_b), (_, _, hh_a, hh_b) = where
    first_half = lanes_first_half()
    adx, ady = adx_ref[lax.axis_index("ha")], ady_ref[lax.axis_index("ha")]
    for l in range(2):
        hs[pl.ds(pl.multiple_of((hh_a + l) * 256, 256), 256), :] = rha[pl.ds(l * 256, 256), :]
        hs[pl.ds(pl.multiple_of((hh_b + l) * 256, 256), 256), :] = rhb[pl.ds(l * 256, 256), :]
    hs_turned[...] = pltpu.roll(hs[...], NV, 1)
    for l in range(3):
        part = pl.ds(l * XROW, XROW)
        for ref, got, base, step in (
            (xs, rxa, xh_a, x_dir),
            (xs, rxb, xh_b, x_dir),
            (ys, rya, yh_a, y_dir),
            (ys, ryb, yh_b, y_dir),
        ):
            ref[pl.ds(pl.multiple_of((base + step * l) * XROW, XROW), XROW), :] = got[part, :]
    x_rows = [(x_start + x_dir * i) * XROW for i in range(16)]
    y_rows = [(y_start + y_dir * i) * YROW for i in range(16)]

    def edges(halo, at, rows, offset):
        own = {i: tile(v_ref, rows[i] + offset) for i in (0, 1, 2, 3, 4, 11, 12, 13, 14, 15)}
        ring = [tile(halo, l * XROW + at) for l in range(5)]
        low = upwind(ring[:3] + [own[i] for i in range(5)])
        high = upwind([own[i] for i in range(11, 16)] + ring[3:])
        return list(zip(range(3), low)) + list(zip(range(14, 16), high))

    def along_x(y, _):
        at = y * YROW
        for i, slope in edges(xs, at, x_rows, at):
            put(h_ref, x_rows[i] + at, tile(h_in, x_rows[i] + at) + adx * slope)
        for i in range(3, 14):
            put(h_ref, x_rows[i] + at, tile(h_in, x_rows[i] + at))
        return 0

    lax.fori_loop(0, 16, along_x, 0)

    def along_y(x, _):
        for i, slope in edges(ys, x * YROW, y_rows, x * XROW):
            row = y_rows[i] + x * XROW
            put(h_ref, row, tile(h_ref, row) + ady * slope)
        return 0

    lax.fori_loop(0, 16, along_y, 0)

    def along_h(n, _):
        at = [pl.ds(n * 64 + p, 8, stride=8) for p in range(8)]
        own = [v_ref[a, :] for a in at]
        own_turned = [turned_ref[a, :] for a in at]
        ring = [tile(hs, l * 256 + n * 8) for l in range(4)]
        ring_turned = [tile(hs_turned, l * 256 + n * 8) for l in range(4)]
        low = heading_terms(ring[:2] + own[:4], ring_turned[:2] + own_turned[:4], first_half)
        high = heading_terms(own[4:] + ring[2:], own_turned[4:] + ring_turned[2:], first_half)
        for p in range(8):
            total = h_ref[at[p], :]
            if p < 2:
                total = total + low[p]
            if p > 5:
                total = total + high[p - 6]
            value = own[p] - DT * jnp.maximum(total, 0.0)
            out_ref[at[p], :] = value
            if last:
                others[0][native(n // 2, lax.rem(n, 2), p)] = value
        return 0

    lax.fori_loop(0, 32, along_h, 0)
    if not last:
        write_faces(where, out_ref, others)


def call(body, name, outs, in_specs, scratch=(), flops=0, moved=4 << 20):
    return pl.pallas_call(
        body,
        name=name,
        out_shape=[jax.ShapeDtypeStruct(s, F32) for s in outs],
        in_specs=in_specs,
        out_specs=[VMEM] * len(outs),
        scratch_shapes=[pltpu.VMEM(s, F32) for s in scratch],
        cost_estimate=pl.CostEstimate(flops=flops, bytes_accessed=moved, transcendentals=0),
        compiler_params=pltpu.CompilerParams(vmem_limit_bytes=8 << 20),
    )


FACES = [(3 * XROW, 128)] * 4 + [(512, 128)] * 2
BLOCK = (ROWS, 128)


def exchange(faces):
    sides = (("gx", 0, False), ("gx", 1, False), ("gy", 0, False), ("gy", 1, False), ("ha", 0, True), ("ha", 1, True))
    arrived = []
    for face, (axis, offset, closed) in zip(faces, sides):
        count = lax.axis_size(axis)
        pairs = []
        for i in range(offset, count if closed else count - 1, 2):
            pairs += [(i, (i + 1) % count), ((i + 1) % count, i)]
        arrived.append(lax.ppermute(face, axis, pairs))
    return arrived


def drift_tables(blocks):
    angle = np.arange(blocks * CH) * (2.0 * np.pi / (blocks * CH))
    speeds = 0.5 + np.arange(NV) / (NV - 1)
    tables, signs = [], []
    for part in (np.cos(angle), np.sin(angle)):
        part = np.where(np.abs(part) < 1e-12, 0.0, part).reshape(blocks, CH)
        positive = (part >= 0).all(axis=1)
        assert (positive | (part <= 0).all(axis=1)).all()
        tables.append(np.abs(part[:, :, None] * speeds).reshape(blocks, PAIRS, 2 * NV).astype(np.float32))
        signs.append(np.where(positive, 1, -1))
    return tables, signs


def steps(initial_value, rows, reads):
    tables, signs = drift_tables(lax.axis_size("ha"))
    adx, ady = (jnp.asarray(t) for t in tables)
    value, *faces = call(
        functools.partial(first_kernel, signs), "first", [BLOCK] + FACES, [VMEM, ANY, ANY]
    )(initial_value, rows, reads)
    for step in range(STEPS):
        last = step == STEPS - 1
        arrived = exchange(faces)
        part, turned = call(
            functools.partial(inner_kernel, signs), "inner", [BLOCK] * 2, [VMEM] * 3, moved=0, flops=100_000_000_000
        )(value, adx, ady)
        value, *faces = call(
            functools.partial(outer_kernel, signs, last),
            "outer",
            [BLOCK] + ([initial_value.shape] if last else FACES),
            [VMEM] * 11,
            scratch=[(6 * XROW, 128), (6 * XROW, 128), (1024, 128), (1024, 128), BLOCK],
            flops=15_000_000,
        )(value, part, turned, adx, ady, *arrived)
    return value, faces[0]


def sample_kernel(rows_ref, v_ref, at_ref, w_ref, out_ref, table, picked):
    first_half = lanes_first_half()

    def fill(n, _):
        tiles = [tile(v_ref, n * 256 + 8 * u) for u in range(32)]
        turned = [pltpu.roll(t, NV, 1) for t in tiles]
        for u in range(32):
            between = jnp.where(first_half, turned[u], pltpu.roll(turned[u], 7, 0))
            table[pl.ds(n * 512 + u * 16, 8, stride=2), :] = tiles[u]
            table[pl.ds(n * 512 + u * 16 + 1, 8, stride=2), :] = between
        return 0

    lax.fori_loop(0, 8, fill, 0)

    def pick(n, _):
        for u in range(8):
            s = n * 8 + u
            for j in range(4):
                row = rows_ref[s * 4 + j]
                for q, shift in enumerate((0, CH, CY * CH, CY * CH + CH)):
                    picked[pl.ds((q * 4 + j) * 256 + s, 1), :] = table[pl.ds(row + shift, 1), :]
        return 0

    lax.fori_loop(0, 32, pick, 0)
    lane = lax.broadcasted_iota(jnp.int32, (8, 128), 1)
    masks = [[((lane & 3) == j) & ((lane >> 4) == q) for q in range(4)] for j in range(4)]

    def weigh(n, _):
        for u in range(8):
            group = n * 8 + u
            total = jnp.zeros((8, 128), F32)
            for j in range(4):
                at = tile(at_ref, j * 256 + group * 8)
                for q in range(4):
                    read = jnp.take_along_axis(tile(picked, (q * 4 + j) * 256 + group * 8), at, axis=1)
                    total = jnp.where(masks[j][q], read, total)
            put(table, group * 8, total * tile(w_ref, group * 8))
        return 0

    lax.fori_loop(0, 4, weigh, 0)
    spread = lax.broadcasted_iota(jnp.int32, (128, 128), 0)
    slot = lax.broadcasted_iota(jnp.int32, (128, 128), 1)
    adder = ((spread < 64) & ((spread & 3) == slot)).astype(F32)
    sums = jnp.dot(
        table[pl.ds(0, 256), :], adder, precision=lax.Precision.HIGHEST, preferred_element_type=F32
    )
    out_ref[...] = sums[:, :4]


def local(initial_value, corner, weights):
    slots = corner.shape[1]
    owners = corner.shape[2]
    request = jnp.concatenate(
        [weights.reshape(16 * slots, owners), corner.reshape(slots, owners).astype(F32)], axis=0
    )
    request = jnp.pad(request.T, ((0, 0), (0, 128 - 17 * slots)))
    request = lax.all_to_all(request, ALL, split_axis=0, concat_axis=0, tiled=True)
    codes = jnp.maximum(request[:, 64 : 64 + slots], 0.0).astype(jnp.int32)
    lane = jnp.arange(128, dtype=jnp.int32)
    reads = (codes.T % NV)[:, :, None] + (((lane >> 2) & 1) + NV * ((lane >> 3) & 1))[None, None, :]
    rows = codes.reshape(-1) // NV
    reads = reads.reshape(slots * owners, 128)
    value, final = steps(initial_value, rows, reads)
    (sums,) = call(
        sample_kernel,
        "samples",
        [(owners, slots)],
        [SMEM, VMEM, VMEM, VMEM],
        scratch=[(2 * ROWS, 128), (16 * owners, 128)],
    )(rows, value, reads, request)
    sampled = lax.all_to_all(sums, ALL, split_axis=0, concat_axis=0, tiled=True)
    sampled = jnp.where(corner >= 0, sampled.T.reshape(corner.shape), 0.0)
    return final, sampled


def solution(mesh):
    return jax.shard_map(
        local,
        mesh=mesh,
        in_specs=(
            P("gx", "gy", "ha"),
            P(("gx", "gy", "ha"), None, None),
            P(("gx", "gy", "ha"), None, None, None),
        ),
        out_specs=(P("gx", "gy", "ha"), P(("gx", "gy", "ha"), None, None)),
        check_vma=False,
    )
```

```python
import functools

import jax
import jax.numpy as jnp
import numpy as np
from jax import lax
from jax.experimental import pallas as pl
from jax.experimental.pallas import tpu as pltpu
from jax.sharding import PartitionSpec as P

NV = 64
STEPS = 4
EPS = 1e-06
DT = 0.15
CX = CY = CH = 16
PAIRS = CH // 2
ROWS = CX * CY * PAIRS
XROW = CY * PAIRS
YROW = PAIRS
F32 = jnp.float32
VMEM = pl.BlockSpec(memory_space=pltpu.VMEM)
ANY = pl.BlockSpec(memory_space=pl.ANY)
SMEM = pl.BlockSpec(memory_space=pltpu.SMEM)
ALL = ("gx", "gy", "ha")

def smooth(low, high, low2, high2, turn):
    mid = (turn * (4.0 / 3.0)) * turn + low * high + EPS
    return mid + high2 * turn, mid, mid - low2 * turn


def inverse(d):
    r = pl.reciprocal(d, approx=True)
    return r * (2.0 - d * r)


def upwind(cells):
    count = len(cells) - 5
    diff = [cells[n + 1] - cells[n] for n in range(count + 4)]
    curve = [diff[n + 1] - diff[n] for n in range(count + 3)]
    turn = [curve[n + 1] - curve[n] for n in range(count + 2)]
    bend = [turn[n] - turn[n + 1] for n in range(count + 1)]
    curve2 = [c + c for c in curve]
    terms = [smooth(curve[n], curve[n + 1], curve2[n], curve2[n + 1], turn[n]) for n in range(count + 2)]
    slopes = []
    for n in range(count):
        a, b, c = terms[n][0], terms[n + 1][1], terms[n + 2][2]
        bc, ac, ab = b * c, a * c, a * b
        alpha, beta, gamma = bc * bc, ac * ac, ab * ab
        gamma3 = 3.0 * gamma
        down = alpha + 6.0 * beta + gamma3
        up = alpha * (bend[n] + bend[n]) + gamma3 * bend[n + 1]
        inner = curve[n + 1] + curve2[n + 2] + up * inverse(down)
        slopes.append(diff[n + 2] + inner * (1.0 / 6.0))
    return slopes


def heading_terms(pairs, turned, first_half):
    count = len(pairs)
    between = [jnp.where(first_half, turned[n], turned[n + 1]) for n in range(count - 1)]
    diff_e = [between[n] - pairs[n] for n in range(count - 1)]
    diff_o = [pairs[n + 1] - between[n] for n in range(count - 1)]
    curve_e = [diff_o[n] - diff_e[n] for n in range(count - 1)]
    curve_o = [diff_e[n + 1] - diff_o[n] for n in range(count - 2)]
    turn_e = [curve_o[n] - curve_e[n] for n in range(count - 2)]
    turn_o = [curve_e[n + 1] - curve_o[n] for n in range(count - 2)]
    two_e, two_o = [c + c for c in curve_e], [c + c for c in curve_o]
    even = [smooth(curve_e[n], curve_o[n], two_e[n], two_o[n], turn_e[n]) for n in range(count - 2)]
    odd = [
        smooth(curve_o[n], curve_e[n + 1], two_o[n], two_e[n + 1], turn_o[n]) for n in range(count - 2)
    ]

    def inner_sum(a, b, c, before, here2, bend_a, bend_c):
        bc, ac, ab = b * c, a * c, a * b
        alpha, beta, gamma = bc * bc, ac * ac, ab * ab
        gamma3 = 3.0 * gamma
        down = alpha + 6.0 * beta + gamma3
        up = alpha * (bend_a + bend_a) + gamma3 * bend_c
        return before + here2 + up * inverse(down)

    result = []
    for n in range(2, count - 2):
        bend_m, bend_0, bend_p = (
            turn_o[n - 2] - turn_e[n - 1],
            turn_e[n - 1] - turn_o[n - 1],
            turn_o[n - 1] - turn_e[n],
        )
        minus = inner_sum(
            odd[n - 2][0], even[n - 1][1], odd[n - 1][2], curve_e[n - 1], two_o[n - 1], bend_m, bend_0
        )
        plus = inner_sum(
            even[n][2], odd[n - 1][1], even[n - 1][0], curve_e[n], two_o[n - 1], bend_p, bend_0
        )
        sixth = 1.0 / 6.0
        result.append(jnp.minimum(diff_o[n - 1] + minus * sixth, plus * sixth - diff_e[n]))
    return result


def tile(ref, row):
    return ref[pl.ds(pl.multiple_of(row, 8), 8), :]


def put(ref, row, value):
    ref[pl.ds(pl.multiple_of(row, 8), 8), :] = value


def lanes_first_half():
    return lax.broadcasted_iota(jnp.int32, (8, 128), 1) < NV


def scalars(signs):
    ha = lax.axis_index("ha")
    found = []
    for axis, sign in (("gx", signs[0]), ("gy", signs[1])):
        even = lax.rem(lax.axis_index(axis), 2) == 0
        wind = jnp.int32(int(sign[0]))
        for block in range(1, len(sign)):
            wind = jnp.where(ha == block, jnp.int32(int(sign[block])), wind)
        ahead = wind > 0
        high, low = jnp.where(ahead, 3, 2), jnp.where(ahead, 0, 5)
        found.append(
            (
                jnp.where(ahead, 0, 15),
                wind,
                jnp.where(even, 13, 0),
                jnp.where(even, 0, 13),
                jnp.where(even, high, low),
                jnp.where(even, low, high),
            )
        )
    even = lax.rem(ha, 2) == 0
    found.append(
        (jnp.where(even, 6, 0), jnp.where(even, 0, 6), jnp.where(even, 2, 0), jnp.where(even, 0, 2))
    )
    return found


def write_faces(where, v_ref, faces):
    (_, _, fx_a, fx_b, _, _), (_, _, fy_a, fy_b, _, _), (fh_a, fh_b, _, _) = where
    fxa, fxb, fya, fyb, fha, fhb = faces

    def body(n, _):
        for l in range(3):
            put(fxa, l * XROW + n * YROW, tile(v_ref, (fx_a + l) * XROW + n * YROW))
            put(fxb, l * XROW + n * YROW, tile(v_ref, (fx_b + l) * XROW + n * YROW))
            put(fya, l * XROW + n * YROW, tile(v_ref, n * XROW + (fy_a + l) * YROW))
            put(fyb, l * XROW + n * YROW, tile(v_ref, n * XROW + (fy_b + l) * YROW))
        for l in range(2):
            for t in range(2):
                base = n * XROW + t * 64
                out = (l * 32 + n * 2 + t) * 8
                put(fha, out, v_ref[pl.ds(base + fh_a + l, 8, stride=8), :])
                put(fhb, out, v_ref[pl.ds(base + fh_b + l, 8, stride=8), :])
        return 0

    lax.fori_loop(0, 16, body, 0, unroll=2)


def native(x, t, p):
    return x, pl.ds(8 * t, 8), pl.ds(128 * p, 128)


def first_kernel(signs, in_ref, rows_ref, reads_ref, v_ref, *faces):
    def body(x, _):
        for t in range(2):
            for p in range(8):
                v_ref[pl.ds(x * XROW + t * 64 + p, 8, stride=8), :] = in_ref[native(x, t, p)]
        return 0

    lax.fori_loop(0, 16, body, 0)
    write_faces(scalars(signs), v_ref, faces)


def inner_kernel(signs, v_ref, adx_ref, ady_ref, h_ref, turned_ref):
    (x_start, x_dir, *_), (y_start, y_dir, *_), _ = scalars(signs)
    first_half = lanes_first_half()
    adx, ady = adx_ref[lax.axis_index("ha")], ady_ref[lax.axis_index("ha")]
    zero = jnp.zeros((8, 128), F32)
    turned_ref[...] = pltpu.roll(v_ref[...], NV, 1)
    xs = [(x_start + x_dir * i) * XROW for i in range(16)]
    ys = [(y_start + y_dir * i) * YROW for i in range(16)]

    def along_x(y, _):
        slopes = upwind([tile(v_ref, row + y * YROW) for row in xs])
        for i in range(16):
            put(h_ref, xs[i] + y * YROW, adx * slopes[i - 3] if 3 <= i <= 13 else zero)
        return 0

    lax.fori_loop(0, 16, along_x, 0)

    def along_y(x, _):
        slopes = upwind([tile(v_ref, row + x * XROW) for row in ys])
        for i in range(3, 14):
            row = ys[i] + x * XROW
            put(h_ref, row, tile(h_ref, row) + ady * slopes[i - 3])
        return 0

    lax.fori_loop(0, 16, along_y, 0)

    def along_h(n, _):
        at = [pl.ds(n * 64 + p, 8, stride=8) for p in range(8)]
        terms = heading_terms([v_ref[a, :] for a in at], [turned_ref[a, :] for a in at], first_half)
        for a, term in zip(at[2:6], terms):
            h_ref[a, :] = h_ref[a, :] + term
        return 0

    lax.fori_loop(0, 32, along_h, 0)


def outer_kernel(
    signs, last, v_ref, h_in, turned_ref, adx_ref, ady_ref, rxb, rxa, rya, ryb, rha, rhb, *rest
):
    out_ref, others = rest[0], rest[1:-5]
    xs, ys, hs, hs_turned, h_ref = rest[-5:]
    where = scalars(signs)
    (x_start, x_dir, _, _, xh_a, xh_b), (y_start, y_dir, _, _, yh_a, yh_b), (_, _, hh_a, hh_b) = where
    first_half = lanes_first_half()
    adx, ady = adx_ref[lax.axis_index("ha")], ady_ref[lax.axis_index("ha")]
    for l in range(2):
        hs[pl.ds(pl.multiple_of((hh_a + l) * 256, 256), 256), :] = rha[pl.ds(l * 256, 256), :]
        hs[pl.ds(pl.multiple_of((hh_b + l) * 256, 256), 256), :] = rhb[pl.ds(l * 256, 256), :]
    hs_turned[...] = pltpu.roll(hs[...], NV, 1)
    for l in range(3):
        part = pl.ds(l * XROW, XROW)
        for ref, got, base, step in (
            (xs, rxa, xh_a, x_dir),
            (xs, rxb, xh_b, x_dir),
            (ys, rya, yh_a, y_dir),
            (ys, ryb, yh_b, y_dir),
        ):
            ref[pl.ds(pl.multiple_of((base + step * l) * XROW, XROW), XROW), :] = got[part, :]
    x_rows = [(x_start + x_dir * i) * XROW for i in range(16)]
    y_rows = [(y_start + y_dir * i) * YROW for i in range(16)]

    def edges(halo, at, rows, offset):
        own = {i: tile(v_ref, rows[i] + offset) for i in (0, 1, 2, 3, 4, 11, 12, 13, 14, 15)}
        ring = [tile(halo, l * XROW + at) for l in range(5)]
        low = upwind(ring[:3] + [own[i] for i in range(5)])
        high = upwind([own[i] for i in range(11, 16)] + ring[3:])
        return list(zip(range(3), low)) + list(zip(range(14, 16), high))

    def along_x(y, _):
        at = y * YROW
        for i, slope in edges(xs, at, x_rows, at):
            put(h_ref, x_rows[i] + at, tile(h_in, x_rows[i] + at) + adx * slope)
        for i in range(3, 14):
            put(h_ref, x_rows[i] + at, tile(h_in, x_rows[i] + at))
        return 0

    lax.fori_loop(0, 16, along_x, 0)

    def along_y(x, _):
        for i, slope in edges(ys, x * YROW, y_rows, x * XROW):
            row = y_rows[i] + x * XROW
            put(h_ref, row, tile(h_ref, row) + ady * slope)
        return 0

    lax.fori_loop(0, 16, along_y, 0)

    def along_h(n, _):
        at = [pl.ds(n * 64 + p, 8, stride=8) for p in range(8)]
        own = [v_ref[a, :] for a in at]
        own_turned = [turned_ref[a, :] for a in at]
        ring = [tile(hs, l * 256 + n * 8) for l in range(4)]
        ring_turned = [tile(hs_turned, l * 256 + n * 8) for l in range(4)]
        low = heading_terms(ring[:2] + own[:4], ring_turned[:2] + own_turned[:4], first_half)
        high = heading_terms(own[4:] + ring[2:], own_turned[4:] + ring_turned[2:], first_half)
        for p in range(8):
            total = h_ref[at[p], :]
            if p < 2:
                total = total + low[p]
            if p > 5:
                total = total + high[p - 6]
            value = own[p] - DT * jnp.maximum(total, 0.0)
            out_ref[at[p], :] = value
            if last:
                others[0][native(n // 2, lax.rem(n, 2), p)] = value
        return 0

    lax.fori_loop(0, 32, along_h, 0)
    if not last:
        write_faces(where, out_ref, others)


def call(body, name, outs, in_specs, scratch=(), flops=0, moved=4 << 20):
    return pl.pallas_call(
        body,
        name=name,
        out_shape=[jax.ShapeDtypeStruct(s, F32) for s in outs],
        in_specs=in_specs,
        out_specs=[VMEM] * len(outs),
        scratch_shapes=[pltpu.VMEM(s, F32) for s in scratch],
        cost_estimate=pl.CostEstimate(flops=flops, bytes_accessed=moved, transcendentals=0),
        compiler_params=pltpu.CompilerParams(vmem_limit_bytes=8 << 20),
    )


FACES = [(3 * XROW, 128)] * 4 + [(512, 128)] * 2
BLOCK = (ROWS, 128)


def exchange(faces):
    sides = (("gx", 0, False), ("gx", 1, False), ("gy", 0, False), ("gy", 1, False), ("ha", 0, True), ("ha", 1, True))
    arrived = []
    for face, (axis, offset, closed) in zip(faces, sides):
        count = lax.axis_size(axis)
        pairs = []
        for i in range(offset, count if closed else count - 1, 2):
            pairs += [(i, (i + 1) % count), ((i + 1) % count, i)]
        arrived.append(lax.ppermute(face, axis, pairs))
    return arrived


def drift_tables(blocks):
    angle = np.arange(blocks * CH) * (2.0 * np.pi / (blocks * CH))
    speeds = 0.5 + np.arange(NV) / (NV - 1)
    tables, signs = [], []
    for part in (np.cos(angle), np.sin(angle)):
        part = np.where(np.abs(part) < 1e-12, 0.0, part).reshape(blocks, CH)
        positive = (part >= 0).all(axis=1)
        assert (positive | (part <= 0).all(axis=1)).all()
        tables.append(np.abs(part[:, :, None] * speeds).reshape(blocks, PAIRS, 2 * NV).astype(np.float32))
        signs.append(np.where(positive, 1, -1))
    return tables, signs


def steps(initial_value, rows, reads):
    tables, signs = drift_tables(lax.axis_size("ha"))
    adx, ady = (jnp.asarray(t) for t in tables)
    value, *faces = call(
        functools.partial(first_kernel, signs), "first", [BLOCK] + FACES, [VMEM, ANY, ANY]
    )(initial_value, rows, reads)
    for step in range(STEPS):
        last = step == STEPS - 1
        arrived = exchange(faces)
        part, turned = call(
            functools.partial(inner_kernel, signs), "inner", [BLOCK] * 2, [VMEM] * 3, moved=0, flops=100_000_000_000
        )(value, adx, ady)
        value, *faces = call(
            functools.partial(outer_kernel, signs, last),
            "outer",
            [BLOCK] + ([initial_value.shape] if last else FACES),
            [VMEM] * 11,
            scratch=[(6 * XROW, 128), (6 * XROW, 128), (1024, 128), (1024, 128), BLOCK],
            flops=15_000_000,
        )(value, part, turned, adx, ady, *(arrived[n] for n in (1, 0, 2, 3, 4, 5)))
    return value, faces[0]


def sample_kernel(rows_ref, v_ref, at_ref, w_ref, out_ref, table, picked):
    first_half = lanes_first_half()

    def fill(n, _):
        tiles = [tile(v_ref, n * 256 + 8 * u) for u in range(32)]
        turned = [pltpu.roll(t, NV, 1) for t in tiles]
        for u in range(32):
            between = jnp.where(first_half, turned[u], pltpu.roll(turned[u], 7, 0))
            table[pl.ds(n * 512 + u * 16, 8, stride=2), :] = tiles[u]
            table[pl.ds(n * 512 + u * 16 + 1, 8, stride=2), :] = between
        return 0

    lax.fori_loop(0, 8, fill, 0)

    def pick(n, _):
        for u in range(8):
            s = n * 8 + u
            for j in range(4):
                row = rows_ref[s * 4 + j]
                for q, shift in enumerate((0, CH, CY * CH, CY * CH + CH)):
                    picked[pl.ds((q * 4 + j) * 256 + s, 1), :] = table[pl.ds(row + shift, 1), :]
        return 0

    lax.fori_loop(0, 32, pick, 0)
    lane = lax.broadcasted_iota(jnp.int32, (8, 128), 1)
    masks = [[((lane & 3) == j) & ((lane >> 4) == q) for q in range(4)] for j in range(4)]

    def weigh(n, _):
        for u in range(8):
            group = n * 8 + u
            total = jnp.zeros((8, 128), F32)
            for j in range(4):
                at = tile(at_ref, j * 256 + group * 8)
                for q in range(4):
                    read = jnp.take_along_axis(tile(picked, (q * 4 + j) * 256 + group * 8), at, axis=1)
                    total = jnp.where(masks[j][q], read, total)
            put(table, group * 8, total * tile(w_ref, group * 8))
        return 0

    lax.fori_loop(0, 4, weigh, 0)
    spread = lax.broadcasted_iota(jnp.int32, (128, 128), 0)
    slot = lax.broadcasted_iota(jnp.int32, (128, 128), 1)
    adder = ((spread < 64) & ((spread & 3) == slot)).astype(F32)
    sums = jnp.dot(
        table[pl.ds(0, 256), :], adder, precision=lax.Precision.HIGHEST, preferred_element_type=F32
    )
    out_ref[...] = sums[:, :4]


def local(initial_value, corner, weights):
    slots = corner.shape[1]
    owners = corner.shape[2]
    request = jnp.concatenate(
        [weights.reshape(16 * slots, owners), corner.reshape(slots, owners).astype(F32)], axis=0
    )
    request = jnp.pad(request.T, ((0, 0), (0, 128 - 17 * slots)))
    request = lax.all_to_all(request, ALL, split_axis=0, concat_axis=0, tiled=True)
    codes = jnp.maximum(request[:, 64 : 64 + slots], 0.0).astype(jnp.int32)
    lane = jnp.arange(128, dtype=jnp.int32)
    reads = (codes.T % NV)[:, :, None] + (((lane >> 2) & 1) + NV * ((lane >> 3) & 1))[None, None, :]
    rows = codes.reshape(-1) // NV
    reads = reads.reshape(slots * owners, 128)
    value, final = steps(initial_value, rows, reads)
    (sums,) = call(
        sample_kernel,
        "samples",
        [(owners, slots)],
        [SMEM, VMEM, VMEM, VMEM],
        scratch=[(2 * ROWS, 128), (16 * owners, 128)],
    )(rows, value, reads, request)
    sampled = lax.all_to_all(sums, ALL, split_axis=0, concat_axis=0, tiled=True)
    sampled = jnp.where(corner >= 0, sampled.T.reshape(corner.shape), 0.0)
    return final, sampled


def solution(mesh):
    return jax.shard_map(
        local,
        mesh=mesh,
        in_specs=(
            P("gx", "gy", "ha"),
            P(("gx", "gy", "ha"), None, None),
            P(("gx", "gy", "ha"), None, None, None),
        ),
        out_specs=(P("gx", "gy", "ha"), P(("gx", "gy", "ha"), None, None)),
        check_vma=False,
    )
```

```python
import functools

import jax
import jax.numpy as jnp
import numpy as np
from jax import lax
from jax.experimental import pallas as pl
from jax.experimental.pallas import tpu as pltpu
from jax.sharding import PartitionSpec as P

NV = 64
STEPS = 4
EPS = 1e-06
DT = 0.15
CX = CY = CH = 16
PAIRS = CH // 2
ROWS = CX * CY * PAIRS
XROW = CY * PAIRS
YROW = PAIRS
F32 = jnp.float32
VMEM = pl.BlockSpec(memory_space=pltpu.VMEM)
ANY = pl.BlockSpec(memory_space=pl.ANY)
SMEM = pl.BlockSpec(memory_space=pltpu.SMEM)
ALL = ("gx", "gy", "ha")

def smooth(low, high, low2, high2, turn):
    mid = (turn * (4.0 / 3.0)) * turn + low * high + EPS
    return mid + high2 * turn, mid, mid - low2 * turn


def inverse(d):
    r = pl.reciprocal(d, approx=True)
    return r * (2.0 - d * r)


def upwind(cells):
    count = len(cells) - 5
    diff = [cells[n + 1] - cells[n] for n in range(count + 4)]
    curve = [diff[n + 1] - diff[n] for n in range(count + 3)]
    turn = [curve[n + 1] - curve[n] for n in range(count + 2)]
    bend = [turn[n] - turn[n + 1] for n in range(count + 1)]
    curve2 = [c + c for c in curve]
    terms = [smooth(curve[n], curve[n + 1], curve2[n], curve2[n + 1], turn[n]) for n in range(count + 2)]
    slopes = []
    for n in range(count):
        a, b, c = terms[n][0], terms[n + 1][1], terms[n + 2][2]
        bc, ac, ab = b * c, a * c, a * b
        alpha, beta, gamma = bc * bc, ac * ac, ab * ab
        gamma3 = 3.0 * gamma
        down = alpha + 6.0 * beta + gamma3
        up = alpha * (bend[n] + bend[n]) + gamma3 * bend[n + 1]
        inner = curve[n + 1] + curve2[n + 2] + up * inverse(down)
        slopes.append(diff[n + 2] + inner * (1.0 / 6.0))
    return slopes


def heading_terms(pairs, turned, first_half):
    count = len(pairs)
    between = [jnp.where(first_half, turned[n], turned[n + 1]) for n in range(count - 1)]
    diff_e = [between[n] - pairs[n] for n in range(count - 1)]
    diff_o = [pairs[n + 1] - between[n] for n in range(count - 1)]
    curve_e = [diff_o[n] - diff_e[n] for n in range(count - 1)]
    curve_o = [diff_e[n + 1] - diff_o[n] for n in range(count - 2)]
    turn_e = [curve_o[n] - curve_e[n] for n in range(count - 2)]
    turn_o = [curve_e[n + 1] - curve_o[n] for n in range(count - 2)]
    two_e, two_o = [c + c for c in curve_e], [c + c for c in curve_o]
    even = [smooth(curve_e[n], curve_o[n], two_e[n], two_o[n], turn_e[n]) for n in range(count - 2)]
    odd = [
        smooth(curve_o[n], curve_e[n + 1], two_o[n], two_e[n + 1], turn_o[n]) for n in range(count - 2)
    ]

    def inner_sum(a, b, c, before, here2, bend_a, bend_c):
        bc, ac, ab = b * c, a * c, a * b
        alpha, beta, gamma = bc * bc, ac * ac, ab * ab
        gamma3 = 3.0 * gamma
        down = alpha + 6.0 * beta + gamma3
        up = alpha * (bend_a + bend_a) + gamma3 * bend_c
        return before + here2 + up * inverse(down)

    result = []
    for n in range(2, count - 2):
        bend_m, bend_0, bend_p = (
            turn_o[n - 2] - turn_e[n - 1],
            turn_e[n - 1] - turn_o[n - 1],
            turn_o[n - 1] - turn_e[n],
        )
        minus = inner_sum(
            odd[n - 2][0], even[n - 1][1], odd[n - 1][2], curve_e[n - 1], two_o[n - 1], bend_m, bend_0
        )
        plus = inner_sum(
            even[n][2], odd[n - 1][1], even[n - 1][0], curve_e[n], two_o[n - 1], bend_p, bend_0
        )
        sixth = 1.0 / 6.0
        result.append(jnp.minimum(diff_o[n - 1] + minus * sixth, plus * sixth - diff_e[n]))
    return result


def tile(ref, row):
    return ref[pl.ds(pl.multiple_of(row, 8), 8), :]


def put(ref, row, value):
    ref[pl.ds(pl.multiple_of(row, 8), 8), :] = value


def lanes_first_half():
    return lax.broadcasted_iota(jnp.int32, (8, 128), 1) < NV


def scalars(signs):
    ha = lax.axis_index("ha")
    found = []
    for axis, sign in (("gx", signs[0]), ("gy", signs[1])):
        even = lax.rem(lax.axis_index(axis), 2) == 0
        wind = jnp.int32(int(sign[0]))
        for block in range(1, len(sign)):
            wind = jnp.where(ha == block, jnp.int32(int(sign[block])), wind)
        ahead = wind > 0
        high, low = jnp.where(ahead, 3, 2), jnp.where(ahead, 0, 5)
        found.append(
            (
                jnp.where(ahead, 0, 15),
                wind,
                jnp.where(even, 13, 0),
                jnp.where(even, 0, 13),
                jnp.where(even, high, low),
                jnp.where(even, low, high),
            )
        )
    even = lax.rem(ha, 2) == 0
    found.append(
        (jnp.where(even, 6, 0), jnp.where(even, 0, 6), jnp.where(even, 2, 0), jnp.where(even, 0, 2))
    )
    return found


def write_faces(where, v_ref, faces):
    (_, _, fx_a, fx_b, _, _), (_, _, fy_a, fy_b, _, _), (fh_a, fh_b, _, _) = where
    fxa, fxb, fya, fyb, fha, fhb = faces

    def body(n, _):
        for l in range(3):
            put(fxa, l * XROW + n * YROW, tile(v_ref, (fx_a + l) * XROW + n * YROW))
            put(fxb, l * XROW + n * YROW, tile(v_ref, (fx_b + l) * XROW + n * YROW))
            put(fya, l * XROW + n * YROW, tile(v_ref, n * XROW + (fy_a + l) * YROW))
            put(fyb, l * XROW + n * YROW, tile(v_ref, n * XROW + (fy_b + l) * YROW))
        for l in range(2):
            for t in range(2):
                base = n * XROW + t * 64
                out = (l * 32 + n * 2 + t) * 8
                put(fha, out, v_ref[pl.ds(base + fh_a + l, 8, stride=8), :])
                put(fhb, out, v_ref[pl.ds(base + fh_b + l, 8, stride=8), :])
        return 0

    lax.fori_loop(0, 16, body, 0, unroll=2)


def native(x, t, p):
    return x, pl.ds(8 * t, 8), pl.ds(128 * p, 128)


def first_kernel(signs, in_ref, rows_ref, reads_ref, v_ref, *faces):
    def body(x, _):
        for t in range(2):
            for p in range(8):
                v_ref[pl.ds(x * XROW + t * 64 + p, 8, stride=8), :] = in_ref[native(x, t, p)]
        return 0

    lax.fori_loop(0, 16, body, 0)
    write_faces(scalars(signs), v_ref, faces)


def inner_kernel(signs, v_ref, adx_ref, ady_ref, h_ref, turned_ref):
    (x_start, x_dir, *_), (y_start, y_dir, *_), _ = scalars(signs)
    first_half = lanes_first_half()
    adx, ady = adx_ref[lax.axis_index("ha")], ady_ref[lax.axis_index("ha")]
    zero = jnp.zeros((8, 128), F32)
    turned_ref[...] = pltpu.roll(v_ref[...], NV, 1)
    xs = [(x_start + x_dir * i) * XROW for i in range(16)]
    ys = [(y_start + y_dir * i) * YROW for i in range(16)]

    def along_x(y, _):
        slopes = upwind([tile(v_ref, row + y * YROW) for row in xs])
        for i in range(16):
            put(h_ref, xs[i] + y * YROW, adx * slopes[i - 3] if 3 <= i <= 13 else zero)
        return 0

    lax.fori_loop(0, 16, along_x, 0)

    def along_y(x, _):
        slopes = upwind([tile(v_ref, row + x * XROW) for row in ys])
        for i in range(3, 14):
            row = ys[i] + x * XROW
            put(h_ref, row, tile(h_ref, row) + ady * slopes[i - 3])
        return 0

    lax.fori_loop(0, 16, along_y, 0)

    def along_h(n, _):
        at = [pl.ds(n * 64 + p, 8, stride=8) for p in range(8)]
        terms = heading_terms([v_ref[a, :] for a in at], [turned_ref[a, :] for a in at], first_half)
        for a, term in zip(at[2:6], terms):
            h_ref[a, :] = h_ref[a, :] + term
        return 0

    lax.fori_loop(0, 32, along_h, 0)


def outer_kernel(
    signs, last, v_ref, h_in, turned_ref, adx_ref, ady_ref, rxa, rxb, ryb, rya, rha, rhb, *rest
):
    out_ref, others = rest[0], rest[1:-5]
    xs, ys, hs, hs_turned, h_ref = rest[-5:]
    where = scalars(signs)
    (x_start, x_dir, _, _, xh_a, xh_b), (y_start, y_dir, _, _, yh_a, yh_b), (_, _, hh_a, hh_b) = where
    first_half = lanes_first_half()
    adx, ady = adx_ref[lax.axis_index("ha")], ady_ref[lax.axis_index("ha")]
    for l in range(2):
        hs[pl.ds(pl.multiple_of((hh_a + l) * 256, 256), 256), :] = rha[pl.ds(l * 256, 256), :]
        hs[pl.ds(pl.multiple_of((hh_b + l) * 256, 256), 256), :] = rhb[pl.ds(l * 256, 256), :]
    hs_turned[...] = pltpu.roll(hs[...], NV, 1)
    for l in range(3):
        part = pl.ds(l * XROW, XROW)
        for ref, got, base, step in (
            (xs, rxa, xh_a, x_dir),
            (xs, rxb, xh_b, x_dir),
            (ys, rya, yh_a, y_dir),
            (ys, ryb, yh_b, y_dir),
        ):
            ref[pl.ds(pl.multiple_of((base + step * l) * XROW, XROW), XROW), :] = got[part, :]
    x_rows = [(x_start + x_dir * i) * XROW for i in range(16)]
    y_rows = [(y_start + y_dir * i) * YROW for i in range(16)]

    def edges(halo, at, rows, offset):
        own = {i: tile(v_ref, rows[i] + offset) for i in (0, 1, 2, 3, 4, 11, 12, 13, 14, 15)}
        ring = [tile(halo, l * XROW + at) for l in range(5)]
        low = upwind(ring[:3] + [own[i] for i in range(5)])
        high = upwind([own[i] for i in range(11, 16)] + ring[3:])
        return list(zip(range(3), low)) + list(zip(range(14, 16), high))

    def along_x(y, _):
        at = y * YROW
        for i, slope in edges(xs, at, x_rows, at):
            put(h_ref, x_rows[i] + at, tile(h_in, x_rows[i] + at) + adx * slope)
        for i in range(3, 14):
            put(h_ref, x_rows[i] + at, tile(h_in, x_rows[i] + at))
        return 0

    lax.fori_loop(0, 16, along_x, 0)

    def along_y(x, _):
        for i, slope in edges(ys, x * YROW, y_rows, x * XROW):
            row = y_rows[i] + x * XROW
            put(h_ref, row, tile(h_ref, row) + ady * slope)
        return 0

    lax.fori_loop(0, 16, along_y, 0)

    def along_h(n, _):
        at = [pl.ds(n * 64 + p, 8, stride=8) for p in range(8)]
        own = [v_ref[a, :] for a in at]
        own_turned = [turned_ref[a, :] for a in at]
        ring = [tile(hs, l * 256 + n * 8) for l in range(4)]
        ring_turned = [tile(hs_turned, l * 256 + n * 8) for l in range(4)]
        low = heading_terms(ring[:2] + own[:4], ring_turned[:2] + own_turned[:4], first_half)
        high = heading_terms(own[4:] + ring[2:], own_turned[4:] + ring_turned[2:], first_half)
        for p in range(8):
            total = h_ref[at[p], :]
            if p < 2:
                total = total + low[p]
            if p > 5:
                total = total + high[p - 6]
            value = own[p] - DT * jnp.maximum(total, 0.0)
            out_ref[at[p], :] = value
            if last:
                others[0][native(n // 2, lax.rem(n, 2), p)] = value
        return 0

    lax.fori_loop(0, 32, along_h, 0)
    if not last:
        write_faces(where, out_ref, others)


def call(body, name, outs, in_specs, scratch=(), flops=0, moved=4 << 20):
    return pl.pallas_call(
        body,
        name=name,
        out_shape=[jax.ShapeDtypeStruct(s, F32) for s in outs],
        in_specs=in_specs,
        out_specs=[VMEM] * len(outs),
        scratch_shapes=[pltpu.VMEM(s, F32) for s in scratch],
        cost_estimate=pl.CostEstimate(flops=flops, bytes_accessed=moved, transcendentals=0),
        compiler_params=pltpu.CompilerParams(vmem_limit_bytes=8 << 20),
    )


FACES = [(3 * XROW, 128)] * 4 + [(512, 128)] * 2
BLOCK = (ROWS, 128)


def exchange(faces):
    sides = (("gx", 0, False), ("gx", 1, False), ("gy", 0, False), ("gy", 1, False), ("ha", 0, True), ("ha", 1, True))
    arrived = []
    for face, (axis, offset, closed) in zip(faces, sides):
        count = lax.axis_size(axis)
        pairs = []
        for i in range(offset, count if closed else count - 1, 2):
            pairs += [(i, (i + 1) % count), ((i + 1) % count, i)]
        arrived.append(lax.ppermute(face, axis, pairs))
    return arrived


def drift_tables(blocks):
    angle = np.arange(blocks * CH) * (2.0 * np.pi / (blocks * CH))
    speeds = 0.5 + np.arange(NV) / (NV - 1)
    tables, signs = [], []
    for part in (np.cos(angle), np.sin(angle)):
        part = np.where(np.abs(part) < 1e-12, 0.0, part).reshape(blocks, CH)
        positive = (part >= 0).all(axis=1)
        assert (positive | (part <= 0).all(axis=1)).all()
        tables.append(np.abs(part[:, :, None] * speeds).reshape(blocks, PAIRS, 2 * NV).astype(np.float32))
        signs.append(np.where(positive, 1, -1))
    return tables, signs


def steps(initial_value, rows, reads):
    tables, signs = drift_tables(lax.axis_size("ha"))
    adx, ady = (jnp.asarray(t) for t in tables)
    value, *faces = call(
        functools.partial(first_kernel, signs), "first", [BLOCK] + FACES, [VMEM, ANY, ANY]
    )(initial_value, rows, reads)
    for step in range(STEPS):
        last = step == STEPS - 1
        arrived = exchange(faces)
        part, turned = call(
            functools.partial(inner_kernel, signs), "inner", [BLOCK] * 2, [VMEM] * 3, moved=0, flops=100_000_000_000
        )(value, adx, ady)
        value, *faces = call(
            functools.partial(outer_kernel, signs, last),
            "outer",
            [BLOCK] + ([initial_value.shape] if last else FACES),
            [VMEM] * 11,
            scratch=[(6 * XROW, 128), (6 * XROW, 128), (1024, 128), (1024, 128), BLOCK],
            flops=15_000_000,
        )(value, part, turned, adx, ady, *(arrived[n] for n in (0, 1, 3, 2, 4, 5)))
    return value, faces[0]


def sample_kernel(rows_ref, v_ref, at_ref, w_ref, out_ref, table, picked):
    first_half = lanes_first_half()

    def fill(n, _):
        tiles = [tile(v_ref, n * 256 + 8 * u) for u in range(32)]
        turned = [pltpu.roll(t, NV, 1) for t in tiles]
        for u in range(32):
            between = jnp.where(first_half, turned[u], pltpu.roll(turned[u], 7, 0))
            table[pl.ds(n * 512 + u * 16, 8, stride=2), :] = tiles[u]
            table[pl.ds(n * 512 + u * 16 + 1, 8, stride=2), :] = between
        return 0

    lax.fori_loop(0, 8, fill, 0)

    def pick(n, _):
        for u in range(8):
            s = n * 8 + u
            for j in range(4):
                row = rows_ref[s * 4 + j]
                for q, shift in enumerate((0, CH, CY * CH, CY * CH + CH)):
                    picked[pl.ds((q * 4 + j) * 256 + s, 1), :] = table[pl.ds(row + shift, 1), :]
        return 0

    lax.fori_loop(0, 32, pick, 0)
    lane = lax.broadcasted_iota(jnp.int32, (8, 128), 1)
    masks = [[((lane & 3) == j) & ((lane >> 4) == q) for q in range(4)] for j in range(4)]

    def weigh(n, _):
        for u in range(8):
            group = n * 8 + u
            total = jnp.zeros((8, 128), F32)
            for j in range(4):
                at = tile(at_ref, j * 256 + group * 8)
                for q in range(4):
                    read = jnp.take_along_axis(tile(picked, (q * 4 + j) * 256 + group * 8), at, axis=1)
                    total = jnp.where(masks[j][q], read, total)
            put(table, group * 8, total * tile(w_ref, group * 8))
        return 0

    lax.fori_loop(0, 4, weigh, 0)
    spread = lax.broadcasted_iota(jnp.int32, (128, 128), 0)
    slot = lax.broadcasted_iota(jnp.int32, (128, 128), 1)
    adder = ((spread < 64) & ((spread & 3) == slot)).astype(F32)
    sums = jnp.dot(
        table[pl.ds(0, 256), :], adder, precision=lax.Precision.HIGHEST, preferred_element_type=F32
    )
    out_ref[...] = sums[:, :4]


def local(initial_value, corner, weights):
    slots = corner.shape[1]
    owners = corner.shape[2]
    request = jnp.concatenate(
        [weights.reshape(16 * slots, owners), corner.reshape(slots, owners).astype(F32)], axis=0
    )
    request = jnp.pad(request.T, ((0, 0), (0, 128 - 17 * slots)))
    request = lax.all_to_all(request, ALL, split_axis=0, concat_axis=0, tiled=True)
    codes = jnp.maximum(request[:, 64 : 64 + slots], 0.0).astype(jnp.int32)
    lane = jnp.arange(128, dtype=jnp.int32)
    reads = (codes.T % NV)[:, :, None] + (((lane >> 2) & 1) + NV * ((lane >> 3) & 1))[None, None, :]
    rows = codes.reshape(-1) // NV
    reads = reads.reshape(slots * owners, 128)
    value, final = steps(initial_value, rows, reads)
    (sums,) = call(
        sample_kernel,
        "samples",
        [(owners, slots)],
        [SMEM, VMEM, VMEM, VMEM],
        scratch=[(2 * ROWS, 128), (16 * owners, 128)],
    )(rows, value, reads, request)
    sampled = lax.all_to_all(sums, ALL, split_axis=0, concat_axis=0, tiled=True)
    sampled = jnp.where(corner >= 0, sampled.T.reshape(corner.shape), 0.0)
    return final, sampled


def solution(mesh):
    return jax.shard_map(
        local,
        mesh=mesh,
        in_specs=(
            P("gx", "gy", "ha"),
            P(("gx", "gy", "ha"), None, None),
            P(("gx", "gy", "ha"), None, None, None),
        ),
        out_specs=(P("gx", "gy", "ha"), P(("gx", "gy", "ha"), None, None)),
        check_vma=False,
    )
```
